32 devices in a mesh: rep: 2 (over y), seq: 4 (over z), head: 2 (over x), sub: 2 (over core).
Axes of the slice: x: 2, y: 2, z: 4, core: 2. Of those that a mesh axis runs over, the one named last changes fastest.
Arguments:
- query_in: bfloat16 [8192, 2048], P(('rep', 'seq', 'sub'), 'head'), parts along dimension 0, may hold values from -6 to 6
- key_in: bfloat16 [8192, 2048], P(('rep', 'seq', 'sub'), 'head'), parts along dimension 0, may hold values from -6 to 6
- value_in: bfloat16 [8192, 2048], P(('rep', 'seq', 'sub'), 'head'), parts along dimension 0, may hold values from -6 to 6
- grad_in: bfloat16 [8192, 2048], P(('rep', 'seq', 'sub'), 'head'), parts along dimension 0, may hold values from -0.0078125 to 0.0078125
Outputs:
- query_gradient: bfloat16 [8192, 2048], P(('rep', 'seq', 'sub'), 'head'), parts along dimension 0
- key_gradient: bfloat16 [8192, 2048], P(('rep', 'seq', 'sub'), 'head'), parts along dimension 0
- value_gradient: bfloat16 [8192, 2048], P(('rep', 'seq', 'sub'), 'head'), parts along dimension 0
The draws below stay inside these ranges and needn't reach their ends.
There are 2 independent parts, one for each index of `rep`. The reference program is written for one: setup_inputs(seed, part) draws one part's arguments, and reference() takes and returns one part's arrays. A program takes and returns all parts, laid end to end along the dimension named above; each array names one. Nothing has to cross between parts.
All inputs are finite; a program needn't handle non-finite values.
Results may differ from the reference program's by a relative error of at most 0.0075.
Values sent between devices are 32-bit elements; how exact they have to be, the bound alone decides.
No kernel may reach another device: no remote copies, remote signals or barrier semaphores. Data moves between devices by JAX's collectives and lax.ppermute only.
A program may use at most 128 MiB of HBM per device.

```python
import jax
import jax.numpy as jnp
from jax import lax

H = 16
DH = 128
TOK_DEV = 512
TOKENS = 4096


def shard_levels(key, shape, cuts, least, top_value):
    factor_of, own = 1.0, jax.random.fold_in(key, 6)
    for position, shards_of in cuts:
        draws = jnp.exp(jax.random.uniform(jax.random.fold_in(own, position), (shards_of,), jnp.float32, least / len(cuts), top_value / len(cuts)))
        factor_of = factor_of * jnp.repeat(draws, shape[position] // shards_of).reshape([-1 if axis == position else 1 for axis in range(len(shape))])
    return factor_of


def scatter_about(rng, dims, width, most, split=(), dtype=jnp.bfloat16):
    values = width * jax.random.normal(rng, dims, jnp.float32)
    if split:
        values = values * shard_levels(rng, dims, split, -0.22, 0.18)
    return jnp.clip(values, -most, most).astype(dtype)


def setup_inputs(seed: int = 0, part: int = 0) -> dict:
    key_list = jax.random.split(jax.random.key(seed), 5)
    part_keys = jax.random.split(jax.random.fold_in(key_list[4], part), 5)
    return {
        "query_in": scatter_about(part_keys[0], (TOKENS, H * DH), 1.0, 6.0, ((0, 8), (1, 2))),
        "key_in": scatter_about(part_keys[1], (TOKENS, H * DH), 1.0, 6.0, ((0, 8), (1, 2))),
        "value_in": scatter_about(part_keys[2], (TOKENS, H * DH), 1.0, 6.0, ((0, 8), (1, 2))),
        "grad_in": scatter_about(part_keys[3], (TOKENS, H * DH), (DH * TOKENS) ** -0.5, 0.0078125, ((0, 8), (1, 2))),
    }


def reference(query_in, key_in, value_in, grad_in):
    blocks = TOKENS // TOK_DEV
    highest_precision = lax.Precision.HIGHEST

    def by_block(array):
        return array.reshape(blocks, TOK_DEV, H, DH).astype(jnp.float32)

    query_b = by_block(query_in)
    key_b = by_block(key_in)
    value_b = by_block(value_in)
    grad_b = by_block(grad_in)
    local_state = jnp.einsum('bthk,bthv->bhkv', key_b, value_b, precision=highest_precision)
    local_state_gradient = jnp.einsum('bthk,bthv->bhkv', query_b, grad_b, precision=highest_precision)
    empty_state = jnp.zeros_like(local_state[:1])
    prefix_state = jnp.concatenate([empty_state, jnp.cumsum(local_state, axis=0)[:-1]], axis=0)
    suffix_state_gradient = jnp.concatenate([jnp.cumsum(local_state_gradient[::-1], axis=0)[:-1][::-1], empty_state], axis=0)
    causal = jnp.arange(TOK_DEV)[:, None] >= jnp.arange(TOK_DEV)[None, :]

    def rounded(scores):
        kept = jnp.where(causal, scores, 0.0)
        return lax.optimization_barrier(kept.astype(jnp.bfloat16)).astype(jnp.float32)

    def block_out(items):
        query_by_token, key_by_token, value_by_token, gradient_by_token, earlier_tokens, later_tokens = items
        score_gradient = rounded(jnp.einsum('thd,shd->hts', gradient_by_token, value_by_token, precision=highest_precision))
        attention_logits = rounded(jnp.einsum('thd,shd->hts', query_by_token, key_by_token, precision=highest_precision))
        query_gradient = jnp.einsum('kev,vkl->ekl', score_gradient, key_by_token, precision=highest_precision) + jnp.einsum('clo,lwo->clw', gradient_by_token, earlier_tokens, precision=highest_precision)
        key_gradient = jnp.einsum('oyk,yov->kov', score_gradient, query_by_token, precision=highest_precision) + jnp.einsum('jmq,mgq->jmg', value_by_token, later_tokens, precision=highest_precision)
        value_gradient = jnp.einsum('oyk,yov->kov', attention_logits, gradient_by_token, precision=highest_precision) + jnp.einsum('idx,dxa->ida', key_by_token, later_tokens, precision=highest_precision)
        return (query_gradient.astype(jnp.bfloat16), key_gradient.astype(jnp.bfloat16), value_gradient.astype(jnp.bfloat16))

    out_query, out_key, out_value = lax.map(block_out, (query_b, key_b, value_b, grad_b, prefix_state, suffix_state_gradient))
    return (out_query.reshape(TOKENS, H * DH), out_key.reshape(TOKENS, H * DH), out_value.reshape(TOKENS, H * DH))
```

```python
import functools

import jax
import jax.numpy as jnp
from jax import lax
from jax.experimental import pallas as pl
from jax.experimental.pallas import tpu as pltpu
from jax.sharding import PartitionSpec as P

DH = 128
F32 = jnp.float32
BF16 = jnp.bfloat16
VMEM = pl.BlockSpec(memory_space=pltpu.VMEM)
HBM = pl.BlockSpec(memory_space=pltpu.HBM)
SMEM = pl.BlockSpec(memory_space=pltpu.SMEM)


def product(left, right, left_axis, right_axis):
    return lax.dot_general(
        left, right, (((left_axis,), (right_axis,)), ((), ())), preferred_element_type=F32
    )


def head_columns(head):
    return slice(head * DH, (head + 1) * DH)


def states_kernel(core, q_hbm, k_hbm, v_hbm, g_hbm, q, k, v, g, give, keep, sems):
    copies = [
        pltpu.make_async_copy(source, target, sems.at[i])
        for i, (source, target) in enumerate(zip((q_hbm, k_hbm, v_hbm, g_hbm), (q, k, v, g)))
    ]
    heads = give.shape[0]
    for c in (0, 3, 1, 2):
        copies[c].start()
    is_first = core[0] == 0
    copies[0].wait()
    copies[3].wait()

    def state(left, right, out):
        for h in range(heads):
            c = head_columns(h)
            out[h] = product(left[:, c], right[:, c], 0, 0)

    @pl.when(is_first)
    def _():
        state(q, g, give)

    @pl.when(jnp.logical_not(is_first))
    def _():
        state(q, g, keep)

    copies[1].wait()
    copies[2].wait()

    @pl.when(is_first)
    def _():
        state(k, v, keep)

    @pl.when(jnp.logical_not(is_first))
    def _():
        state(k, v, give)


def states(core, q, k, v, g):
    rows, width = q.shape
    heads = width // DH
    return pl.pallas_call(
        states_kernel,
        in_specs=[SMEM] + [HBM] * 4,
        out_specs=[VMEM] * 6,
        out_shape=[pltpu.VMEM(q.shape, BF16)] * 4 + [pltpu.VMEM((heads, DH, DH), F32)] * 2,
        scratch_shapes=[pltpu.SemaphoreType.DMA((4,))],
        compiler_params=pltpu.CompilerParams(vmem_limit_bytes=8 << 20),
        name="states",
    )(core, *[pltpu.with_memory_space_constraint(x, pltpu.HBM) for x in (q, k, v, g)])


def intra_kernel(first, q, k, v, g, dq, dk, dv):
    rows = q.shape[0]
    row = lax.broadcasted_iota(jnp.int32, (rows, rows), 0)
    col = lax.broadcasted_iota(jnp.int32, (rows, rows), 1)
    for h in range(dq.shape[1] // DH):
        c, o = head_columns(first + h), head_columns(h)
        qh, kh, vh, gh = q[:, c], k[:, c], v[:, c], g[:, c]
        grad_scores = jnp.where(row >= col, product(gh, vh, 1, 1), 0.0).astype(BF16)
        dq[:, o] = product(grad_scores, kh, 1, 0)
        dk[:, o] = product(grad_scores, qh, 0, 0)
        attn_scores = jnp.where(row <= col, product(kh, qh, 1, 1), 0.0).astype(BF16)
        dv[:, o] = product(attn_scores, gh, 1, 0)


def intra(first, heads, q, k, v, g):
    return pl.pallas_call(
        functools.partial(intra_kernel, first),
        in_specs=[VMEM] * 4,
        out_specs=[VMEM] * 3,
        out_shape=[pltpu.VMEM((q.shape[0], heads * DH), F32)] * 3,
        compiler_params=pltpu.CompilerParams(vmem_limit_bytes=16 << 20),
        name="intra",
    )(q, k, v, g)


def final_kernel(core, k, v, g, mine, other, dqi, dki, dvi, dq_hbm, dk_hbm, dv_hbm, dq, dk, dv, sems):
    heads = mine.shape[0]
    is_first = core[0] == 0
    copies = []
    for h in range(heads):
        c = head_columns(h)
        prefix = jnp.where(is_first, mine[h], other[h]).astype(BF16)
        suffix = jnp.where(is_first, other[h], mine[h]).astype(BF16)
        dq[:, c] = (dqi[:, c] + product(g[:, c], prefix, 1, 1)).astype(BF16)
        dk[:, c] = (dki[:, c] + product(v[:, c], suffix, 1, 1)).astype(BF16)
        dv[:, c] = (dvi[:, c] + product(k[:, c], suffix, 1, 0)).astype(BF16)
        if h % 2 == 1 or h == heads - 1:
            cc = slice((h - h % 2) * DH, (h + 1) * DH)
            for i, (source, target) in enumerate(((dq, dq_hbm), (dk, dk_hbm), (dv, dv_hbm))):
                copy = pltpu.make_async_copy(source.at[:, cc], target.at[:, cc], sems.at[i, h // 2])
                copy.start()
                copies.append(copy)
    for copy in copies:
        copy.wait()


def final(core, k, v, g, mine, other, dqi, dki, dvi):
    shape = jax.ShapeDtypeStruct(k.shape, BF16)
    heads = mine.shape[0]
    return pl.pallas_call(
        final_kernel,
        in_specs=[SMEM] + [VMEM] * 8,
        out_specs=[HBM] * 3,
        out_shape=[shape] * 3,
        scratch_shapes=[pltpu.VMEM(k.shape, BF16)] * 3
        + [pltpu.SemaphoreType.DMA((3, (heads + 1) // 2))],
        compiler_params=pltpu.CompilerParams(vmem_limit_bytes=16 << 20),
        name="final",
    )(core, k, v, g, mine, other, dqi, dki, dvi)


def body(query_in, key_in, value_in, grad_in):
    chips = lax.axis_size("seq")
    core = lax.axis_index("sub").astype(jnp.int32).reshape(1)
    heads = query_in.shape[1] // DH
    swap = [(0, 1), (1, 0)]
    q, k, v, g, give, keep = states(core, query_in, key_in, value_in, grad_in)
    total = keep + lax.ppermute(give, "sub", swap)
    mine = None
    arrived = None
    for step in range(chips - 1):
        pairs = [
            (2 * step, 2 * step + 2),
            (2 * (chips - 1 - step) + 1, 2 * (chips - 2 - step) + 1),
        ]
        sent = total if arrived is None else total + arrived
        arrived = lax.ppermute(sent, ("seq", "sub"), pairs)
        mine = arrived if mine is None else mine + arrived
    other = lax.ppermute(mine + keep, "sub", swap)
    dqi, dki, dvi = intra(0, heads, q, k, v, g)
    return tuple(final(core, k, v, g, mine, other, dqi, dki, dvi))


def solution(mesh):
    placed = P(("rep", "seq", "sub"), "head")
    return jax.shard_map(
        body, mesh=mesh, in_specs=(placed,) * 4, out_specs=(placed,) * 3, check_vma=False
    )
```

```python
import functools

import jax
import jax.numpy as jnp
from jax import lax
from jax.experimental import pallas as pl
from jax.experimental.pallas import tpu as pltpu
from jax.sharding import PartitionSpec as P

DH = 128
F32 = jnp.float32
BF16 = jnp.bfloat16
VMEM = pl.BlockSpec(memory_space=pltpu.VMEM)
HBM = pl.BlockSpec(memory_space=pltpu.HBM)
SMEM = pl.BlockSpec(memory_space=pltpu.SMEM)


def product(left, right, left_axis, right_axis):
    return lax.dot_general(
        left, right, (((left_axis,), (right_axis,)), ((), ())), preferred_element_type=F32
    )


def head_columns(head):
    return slice(head * DH, (head + 1) * DH)


def states_kernel(core, q_hbm, k_hbm, v_hbm, g_hbm, q, k, v, g, *rest):
    parts = (len(rest) - 1) // 2
    give, keep, sems = rest[:parts], rest[parts : 2 * parts], rest[-1]
    copies = [
        pltpu.make_async_copy(source, target, sems.at[i])
        for i, (source, target) in enumerate(zip((q_hbm, k_hbm, v_hbm, g_hbm), (q, k, v, g)))
    ]
    for c in (0, 3, 1, 2):
        copies[c].start()
    is_first = core[0] == 0

    def state(left, right, outs):
        h = 0
        for out in outs:
            for i in range(out.shape[0]):
                c = head_columns(h)
                out[i] = product(left[:, c], right[:, c], 0, 0)
                h += 1

    for left, right, give_first in ((0, 3, True), (1, 2, False)):
        copies[left].wait()
        copies[right].wait()
        pair = (q, k, v, g)[left], (q, k, v, g)[right]

        @pl.when(is_first)
        def _():
            state(*pair, give if give_first else keep)

        @pl.when(jnp.logical_not(is_first))
        def _():
            state(*pair, keep if give_first else give)


def states(core, parts, q, k, v, g):
    outs = [pltpu.VMEM((n, DH, DH), F32) for n in parts] * 2
    result = pl.pallas_call(
        states_kernel,
        in_specs=[SMEM] + [HBM] * 4,
        out_specs=[VMEM] * (4 + len(outs)),
        out_shape=[pltpu.VMEM(q.shape, BF16)] * 4 + outs,
        scratch_shapes=[pltpu.SemaphoreType.DMA((4,))],
        compiler_params=pltpu.CompilerParams(vmem_limit_bytes=8 << 20),
        name="states",
    )(core, *[pltpu.with_memory_space_constraint(x, pltpu.HBM) for x in (q, k, v, g)])
    return result[:4], result[4 : 4 + len(parts)], result[4 + len(parts) :]


def intra_kernel(first, q, k, v, g, dq, dk, dv):
    rows = q.shape[0]
    row = lax.broadcasted_iota(jnp.int32, (rows, rows), 0)
    col = lax.broadcasted_iota(jnp.int32, (rows, rows), 1)
    for h in range(dq.shape[1] // DH):
        c, o = head_columns(first + h), head_columns(h)
        qh, kh, vh, gh = q[:, c], k[:, c], v[:, c], g[:, c]
        grad_scores = jnp.where(row >= col, product(gh, vh, 1, 1), 0.0).astype(BF16)
        dq[:, o] = product(grad_scores, kh, 1, 0)
        dk[:, o] = product(grad_scores, qh, 0, 0)
        attn_scores = jnp.where(row <= col, product(kh, qh, 1, 1), 0.0).astype(BF16)
        dv[:, o] = product(attn_scores, gh, 1, 0)


def intra(first, heads, q, k, v, g):
    return pl.pallas_call(
        functools.partial(intra_kernel, first),
        in_specs=[VMEM] * 4,
        out_specs=[VMEM] * 3,
        out_shape=[pltpu.VMEM((q.shape[0], heads * DH), F32)] * 3,
        compiler_params=pltpu.CompilerParams(vmem_limit_bytes=16 << 20),
        name="intra",
    )(q, k, v, g)


def final_kernel(parts, core, k, v, g, *rest):
    count = len(parts)
    mine, other, rest = rest[:count], rest[count : 2 * count], rest[2 * count :]
    local, rest = rest[: 3 * count], rest[3 * count :]
    (targets, outs, sems) = rest[:3], rest[3:6], rest[6]
    is_first = core[0] == 0
    copies = []
    first = 0
    for p in range(count):
        for i in range(parts[p]):
            c, o = head_columns(first + i), head_columns(i)
            prefix = jnp.where(is_first, mine[p][i], other[p][i]).astype(BF16)
            suffix = jnp.where(is_first, other[p][i], mine[p][i]).astype(BF16)
            outs[0][:, c] = (local[3 * p][:, o] + product(g[:, c], prefix, 1, 1)).astype(BF16)
            outs[1][:, c] = (local[3 * p + 1][:, o] + product(v[:, c], suffix, 1, 1)).astype(BF16)
            outs[2][:, c] = (local[3 * p + 2][:, o] + product(k[:, c], suffix, 1, 0)).astype(BF16)
            if i % 2 == 1 or i == parts[p] - 1:
                cc = slice((first + i - i % 2) * DH, (first + i + 1) * DH)
                for n in range(3):
                    copy = pltpu.make_async_copy(
                        outs[n].at[:, cc], targets[n].at[:, cc], sems.at[n, first + i]
                    )
                    copy.start()
                    copies.append(copy)
        first += parts[p]
    for copy in copies:
        copy.wait()


def final(core, parts, k, v, g, mine, other, local):
    shape = jax.ShapeDtypeStruct(k.shape, BF16)
    return pl.pallas_call(
        functools.partial(final_kernel, parts),
        in_specs=[SMEM] + [VMEM] * (3 + 5 * len(parts)),
        out_specs=[HBM] * 3,
        out_shape=[shape] * 3,
        scratch_shapes=[pltpu.VMEM(k.shape, BF16)] * 3
        + [pltpu.SemaphoreType.DMA((3, sum(parts)))],
        compiler_params=pltpu.CompilerParams(vmem_limit_bytes=16 << 20),
        name="final",
    )(core, k, v, g, *mine, *other, *local)


def after(values, *events):
    values = tuple(values)
    return lax.optimization_barrier(values + tuple(events))[: len(values)]


def move(value, chips, hops):
    pairs = []
    for a, b in hops:
        pairs += [(2 * a, 2 * b), (2 * (chips - 1 - a) + 1, 2 * (chips - 1 - b) + 1)]
    return lax.ppermute(value, ("seq", "sub"), pairs)


def body(query_in, key_in, value_in, grad_in):
    chips = lax.axis_size("seq")
    core = lax.axis_index("sub").astype(jnp.int32).reshape(1)
    heads = query_in.shape[1] // DH
    parts = (heads // 2, heads - heads // 2)
    swap = [(0, 1), (1, 0)]
    args, give, keep = states(core, parts, query_in, key_in, value_in, grad_in)
    got = [lax.ppermute(x, "sub", swap) for x in give]
    total_a, total_b = (x + y for x, y in zip(keep, got))
    last = chips - 1
    mine_a = arrived_a = move(total_a, chips, [(0, 1)])
    mine_b = arrived_b = move(total_b, chips, [(0, 1), (last - 1, last)])
    local_a = intra(0, parts[0], *after(args, total_a, total_b))
    (arrived_a,) = after((arrived_a,), local_a[0])
    for hop in range(1, last):
        sent_a = total_a + arrived_a
        arrived_a = move(sent_a, chips, [(hop, hop + 1)])
        if hop < last - 1:
            (arrived_b,) = after((arrived_b,), sent_a)
            sent_b = total_b + arrived_b
            if hop == last - 2:
                mine_b = mine_b + move(sent_b, chips, [(hop, last)])
            arrived_b = move(sent_b, chips, [(hop, hop + 1)])
            if hop < last - 2:
                mine_b = mine_b + arrived_b
        if hop < last - 1:
            mine_a = mine_a + arrived_a
    local_b = intra(parts[0], parts[1], *after(args, sent_a))
    arrived_a, arrived_b = after((arrived_a, arrived_b), local_b[0])
    mine_a = mine_a + arrived_a
    mine_b = mine_b + arrived_b
    other_b = lax.ppermute(mine_b + keep[1], "sub", swap)
    other_a = lax.ppermute(mine_a + keep[0], "sub", swap)
    q, k, v, g = args
    return tuple(
        final(core, parts, k, v, g, (mine_a, mine_b), (other_a, other_b), (*local_a, *local_b))
    )


def solution(mesh):
    placed = P(("rep", "seq", "sub"), "head")
    return jax.shard_map(
        body, mesh=mesh, in_specs=(placed,) * 4, out_specs=(placed,) * 3, check_vma=False
    )
```

```python
import functools

import jax
import jax.numpy as jnp
from jax import lax
from jax.experimental import pallas as pl
from jax.experimental.pallas import tpu as pltpu
from jax.sharding import PartitionSpec as P

DH = 128
LITTLE = pl.CostEstimate(flops=1, transcendentals=0, bytes_accessed=1)
PIECES = (1, 2, 5)
F32 = jnp.float32
BF16 = jnp.bfloat16
VMEM = pl.BlockSpec(memory_space=pltpu.VMEM)
HBM = pl.BlockSpec(memory_space=pltpu.HBM)
SMEM = pl.BlockSpec(memory_space=pltpu.SMEM)


def product(left, right, left_axis, right_axis):
    return lax.dot_general(
        left, right, (((left_axis,), (right_axis,)), ((), ())), preferred_element_type=F32
    )


def head_columns(head):
    return slice(head * DH, (head + 1) * DH)


def states_kernel(aliased, place, q_hbm, k_hbm, v_hbm, g_hbm, *rest):
    rest = rest[aliased:]
    q, k, v, g = rest[:4]
    parts = (len(rest) - 5) // 2
    keep, give, sems = rest[4 : 4 + parts], rest[4 + parts : 4 + 2 * parts], rest[-1]
    copies = [
        pltpu.make_async_copy(source, target, sems.at[i])
        for i, (source, target) in enumerate(zip((q_hbm, k_hbm, v_hbm, g_hbm), (q, k, v, g)))
    ]
    is_first = place[0] == 0

    def state(left, right, outs):
        h = 0
        for out in outs:
            for i in range(out.shape[0]):
                c = head_columns(h)
                out[i] = product(left[:, c], right[:, c], 0, 0)
                h += 1

    @pl.when(place[1] == 1)
    def _():
        for c in (0, 3, 1, 2):
            copies[c].start()
        for left, right, give_first in ((0, 3, True), (1, 2, False)):
            copies[left].wait()
            copies[right].wait()
            pair = (q, k, v, g)[left], (q, k, v, g)[right]

            @pl.when(is_first)
            def _():
                state(*pair, give if give_first else keep)

            @pl.when(jnp.logical_not(is_first))
            def _():
                state(*pair, keep if give_first else give)


def states(core, active, parts, args, filled=()):
    place = jnp.stack([core, active.astype(jnp.int32)])
    outs = [pltpu.VMEM((n, DH, DH), F32) for n in parts]
    result = pl.pallas_call(
        functools.partial(states_kernel, len(filled)),
        in_specs=[SMEM] + [HBM] * 4 + [VMEM] * len(filled),
        out_specs=[VMEM] * (4 + 2 * len(outs)),
        out_shape=[pltpu.VMEM(args[0].shape, BF16)] * 4 + outs + outs,
        scratch_shapes=[pltpu.SemaphoreType.DMA((4,))],
        input_output_aliases={5 + i: i for i in range(len(filled))},
        compiler_params=pltpu.CompilerParams(vmem_limit_bytes=8 << 20),
        name="states",
        cost_estimate=LITTLE,
    )(place, *[pltpu.with_memory_space_constraint(x, pltpu.HBM) for x in args], *filled)
    return result[: 4 + len(parts)], result[4 + len(parts) :]


def intra_kernel(first, q, k, v, g, dq, dk, dv):
    rows = q.shape[0]
    row = lax.broadcasted_iota(jnp.int32, (rows, rows), 0)
    col = lax.broadcasted_iota(jnp.int32, (rows, rows), 1)
    for h in range(dq.shape[1] // DH):
        c, o = head_columns(first + h), head_columns(h)
        qh, kh, vh, gh = q[:, c], k[:, c], v[:, c], g[:, c]
        grad_scores = jnp.where(row >= col, product(gh, vh, 1, 1), 0.0).astype(BF16)
        dq[:, o] = product(grad_scores, kh, 1, 0)
        dk[:, o] = product(grad_scores, qh, 0, 0)
        attn_scores = jnp.where(row <= col, product(kh, qh, 1, 1), 0.0).astype(BF16)
        dv[:, o] = product(attn_scores, gh, 1, 0)


def intra(first, heads, q, k, v, g):
    return pl.pallas_call(
        functools.partial(intra_kernel, first),
        in_specs=[VMEM] * 4,
        out_specs=[VMEM] * 3,
        out_shape=[pltpu.VMEM((q.shape[0], heads * DH), F32)] * 3,
        compiler_params=pltpu.CompilerParams(vmem_limit_bytes=16 << 20),
        name="intra",
        cost_estimate=LITTLE,
    )(q, k, v, g)


def final_kernel(parts, pieces, core, k, v, g, *rest):
    count = len(parts)
    mine, other, rest = rest[:count], rest[count : 2 * count], rest[2 * count :]
    local, rest = rest[: 3 * len(pieces)], rest[3 * len(pieces) :]
    (targets, outs, sems) = rest[:3], rest[3:6], rest[6]
    is_first = core[0] == 0
    of_part = [(p, i) for p, n in enumerate(parts) for i in range(n)]
    of_piece = [(p, i) for p, n in enumerate(pieces) for i in range(n)]
    heads = len(of_part)
    copies = []
    for h in range(heads):
        (part, i), (piece, j) = of_part[h], of_piece[h]
        c, o = head_columns(h), head_columns(j)
        prefix = jnp.where(is_first, mine[part][i], other[part][i]).astype(BF16)
        suffix = jnp.where(is_first, other[part][i], mine[part][i]).astype(BF16)
        local_q, local_k, local_v = (x[:, o] for x in local[3 * piece : 3 * piece + 3])
        outs[0][:, c] = (local_q + product(g[:, c], prefix, 1, 1)).astype(BF16)
        outs[1][:, c] = (local_k + product(v[:, c], suffix, 1, 1)).astype(BF16)
        outs[2][:, c] = (local_v + product(k[:, c], suffix, 1, 0)).astype(BF16)
        if h % 2 == 1 or h == heads - 1:
            cc = slice((h - h % 2) * DH, (h + 1) * DH)
            for n in range(3):
                copy = pltpu.make_async_copy(
                    outs[n].at[:, cc], targets[n].at[:, cc], sems.at[n, h // 2]
                )
                copy.start()
                copies.append(copy)
    for copy in copies:
        copy.wait()


def final(core, parts, pieces, k, v, g, mine, other, local):
    shape = jax.ShapeDtypeStruct(k.shape, BF16)
    return pl.pallas_call(
        functools.partial(final_kernel, parts, pieces),
        in_specs=[SMEM] + [VMEM] * (3 + 2 * len(parts) + 3 * len(pieces)),
        out_specs=[HBM] * 3,
        out_shape=[shape] * 3,
        scratch_shapes=[pltpu.VMEM(k.shape, BF16)] * 3
        + [pltpu.SemaphoreType.DMA((3, (sum(parts) + 1) // 2))],
        compiler_params=pltpu.CompilerParams(vmem_limit_bytes=16 << 20),
        name="final",
        cost_estimate=LITTLE,
    )(core.reshape(1), k, v, g, *mine, *other, *[x for piece in local for x in piece])


def after(values, *events):
    values = tuple(values)
    return lax.optimization_barrier(values + tuple(events))[: len(values)]


def move(value, chips, hops):
    pairs = []
    for a, b in hops:
        pairs += [(2 * a, 2 * b), (2 * (chips - 1 - a) + 1, 2 * (chips - 1 - b) + 1)]
    return lax.ppermute(value, ("seq", "sub"), pairs)


def swap(value, chips=None):
    if chips is None:
        return lax.ppermute(value, "sub", [(0, 1), (1, 0)])
    pairs = [pair for c in chips for pair in ((2 * c, 2 * c + 1), (2 * c + 1, 2 * c))]
    return lax.ppermute(value, ("seq", "sub"), pairs)


def body(*args):
    chips = lax.axis_size("seq")
    last = chips - 1
    ends, middle = (0, last), range(1, last)
    core = lax.axis_index("sub").astype(jnp.int32)
    chip = lax.axis_index("seq")
    at_end = jnp.logical_or(chip == 0, chip == last)
    heads = args[0].shape[1] // DH
    parts = (heads // 2, heads - heads // 2)
    pieces = PIECES if heads == 8 else (1, 1, heads - 2)

    filled, give = states(core, at_end, parts, args)
    got_a, got_b = (swap(x, ends) for x in give)
    first_a, first_b = filled[4] + got_a, filled[5] + got_b
    arrived_a, arrived_b = (move(x, chips, [(0, 1)]) for x in (first_a, first_b))
    filled, give = states(
        core, jnp.logical_not(at_end), parts, args, after(filled, first_a, first_b)
    )
    args, keep = filled[:4], filled[4:]
    total_a, total_b = (x + y + swap(z, middle) for x, y, z in zip(keep, (got_a, got_b), give))
    mine_a, mine_b = arrived_a, arrived_b
    carried_b = move(total_b, chips, [(last - 1, last)])
    local = [intra(0, pieces[0], *after(args, total_a, total_b))]
    (arrived_a,) = after((arrived_a,), local[0][0])
    (arrived_b,) = after((arrived_b,), carried_b)
    mine_b = mine_b + carried_b
    for hop in range(1, last):
        sent_a = total_a + arrived_a
        arrived_a = move(sent_a, chips, [(hop, hop + 1)])
        if hop < last - 1:
            mine_a = mine_a + arrived_a
            if hop == last - 2:
                local.append(intra(pieces[0], pieces[1], *after(args, sent_a)))
                (arrived_b,) = after((arrived_b,), local[1][0])
            else:
                (arrived_b,) = after((arrived_b,), sent_a)
            sent_b = total_b + arrived_b
            if hop == last - 2:
                mine_b = mine_b + move(sent_b, chips, [(hop, last)])
            arrived_b = move(sent_b, chips, [(hop, hop + 1)])
            if hop < last - 2:
                mine_b = mine_b + arrived_b
    local.append(intra(sum(pieces[:2]), pieces[2], *after(args, sent_a)))
    arrived_a, arrived_b = after((arrived_a, arrived_b), local[2][0])
    mine_a = mine_a + arrived_a
    mine_b = mine_b + arrived_b
    other_b = swap(mine_b + keep[1])
    other_a = swap(mine_a + keep[0])
    q, k, v, g = args
    return tuple(final(core, parts, pieces, k, v, g, (mine_a, mine_b), (other_a, other_b), local))


def solution(mesh):
    placed = P(("rep", "seq", "sub"), "head")
    return jax.shard_map(
        body, mesh=mesh, in_specs=(placed,) * 4, out_specs=(placed,) * 3, check_vma=False
    )
```

```python
import functools

import jax
import jax.numpy as jnp
from jax import lax
from jax.experimental import pallas as pl
from jax.experimental.pallas import tpu as pltpu
from jax.sharding import PartitionSpec as P

DH = 128
CHUNKS = 4
PLAN = (1, 1, 1, 0, 1, 1, 1, 2)
F32 = jnp.float32
BF16 = jnp.bfloat16
VMEM = pl.BlockSpec(memory_space=pltpu.VMEM)
HBM = pl.BlockSpec(memory_space=pltpu.HBM)
SMEM = pl.BlockSpec(memory_space=pltpu.SMEM)


def product(left, right, left_axis, right_axis):
    return lax.dot_general(
        left, right, (((left_axis,), (right_axis,)), ((), ())), preferred_element_type=F32
    )


def head_columns(head):
    return slice(head * DH, (head + 1) * DH)


def states_kernel(core, q_hbm, k_hbm, v_hbm, g_hbm, q, k, v, g, *rest):
    parts = (len(rest) - 1) // 2
    give, keep, sems = rest[:parts], rest[parts : 2 * parts], rest[-1]
    copies = [
        pltpu.make_async_copy(source, target, sems.at[i])
        for i, (source, target) in enumerate(zip((q_hbm, k_hbm, v_hbm, g_hbm), (q, k, v, g)))
    ]
    for c in (0, 3, 1, 2):
        copies[c].start()
    is_first = core[0] == 0

    def state(left, right, outs):
        h = 0
        for out in outs:
            for i in range(out.shape[0]):
                c = head_columns(h)
                out[i] = product(left[:, c], right[:, c], 0, 0)
                h += 1

    for left, right, give_first in ((0, 3, True), (1, 2, False)):
        copies[left].wait()
        copies[right].wait()
        pair = (q, k, v, g)[left], (q, k, v, g)[right]

        @pl.when(is_first)
        def _():
            state(*pair, give if give_first else keep)

        @pl.when(jnp.logical_not(is_first))
        def _():
            state(*pair, keep if give_first else give)


def states(core, parts, q, k, v, g):
    outs = [pltpu.VMEM((n, DH, DH), F32) for n in parts] * 2
    result = pl.pallas_call(
        states_kernel,
        in_specs=[SMEM] + [HBM] * 4,
        out_specs=[VMEM] * (4 + len(outs)),
        out_shape=[pltpu.VMEM(q.shape, BF16)] * 4 + outs,
        scratch_shapes=[pltpu.SemaphoreType.DMA((4,))],
        compiler_params=pltpu.CompilerParams(vmem_limit_bytes=8 << 20),
        name="states",
    )(core, *[pltpu.with_memory_space_constraint(x, pltpu.HBM) for x in (q, k, v, g)])
    return result[:4], result[4 : 4 + len(parts)], result[4 + len(parts) :]


def intra_kernel(first, q, k, v, g, dq, dk, dv):
    rows = q.shape[0]
    row = lax.broadcasted_iota(jnp.int32, (rows, rows), 0)
    col = lax.broadcasted_iota(jnp.int32, (rows, rows), 1)
    for h in range(dq.shape[1] // DH):
        c, o = head_columns(first + h), head_columns(h)
        qh, kh, vh, gh = q[:, c], k[:, c], v[:, c], g[:, c]
        grad_scores = jnp.where(row >= col, product(gh, vh, 1, 1), 0.0).astype(BF16)
        dq[:, o] = product(grad_scores, kh, 1, 0)
        dk[:, o] = product(grad_scores, qh, 0, 0)
        attn_scores = jnp.where(row <= col, product(kh, qh, 1, 1), 0.0).astype(BF16)
        dv[:, o] = product(attn_scores, gh, 1, 0)


def intra(first, heads, q, k, v, g):
    return pl.pallas_call(
        functools.partial(intra_kernel, first),
        in_specs=[VMEM] * 4,
        out_specs=[VMEM] * 3,
        out_shape=[pltpu.VMEM((q.shape[0], heads * DH), F32)] * 3,
        compiler_params=pltpu.CompilerParams(vmem_limit_bytes=16 << 20),
        name="intra",
    )(q, k, v, g)


def final_kernel(parts, pieces, core, k, v, g, *rest):
    count = len(parts)
    mine, other, rest = rest[:count], rest[count : 2 * count], rest[2 * count :]
    local, rest = rest[: 3 * len(pieces)], rest[3 * len(pieces) :]
    (targets, outs, sems) = rest[:3], rest[3:6], rest[6]
    is_first = core[0] == 0
    of_part = [(p, i) for p, n in enumerate(parts) for i in range(n)]
    of_piece = [(p, i) for p, n in enumerate(pieces) for i in range(n)]
    heads = len(of_part)
    copies = []
    for h in range(heads):
        (part, i), (piece, j) = of_part[h], of_piece[h]
        c, o = head_columns(h), head_columns(j)
        prefix = jnp.where(is_first, mine[part][i], other[part][i]).astype(BF16)
        suffix = jnp.where(is_first, other[part][i], mine[part][i]).astype(BF16)
        local_q, local_k, local_v = (x[:, o] for x in local[3 * piece : 3 * piece + 3])
        outs[0][:, c] = (local_q + product(g[:, c], prefix, 1, 1)).astype(BF16)
        outs[1][:, c] = (local_k + product(v[:, c], suffix, 1, 1)).astype(BF16)
        outs[2][:, c] = (local_v + product(k[:, c], suffix, 1, 0)).astype(BF16)
        if h % 2 == 1 or h == heads - 1:
            cc = slice((h - h % 2) * DH, (h + 1) * DH)
            for n in range(3):
                copy = pltpu.make_async_copy(
                    outs[n].at[:, cc], targets[n].at[:, cc], sems.at[n, h // 2]
                )
                copy.start()
                copies.append(copy)
    for copy in copies:
        copy.wait()


def final(core, parts, pieces, k, v, g, mine, other, local):
    shape = jax.ShapeDtypeStruct(k.shape, BF16)
    return pl.pallas_call(
        functools.partial(final_kernel, parts, pieces),
        in_specs=[SMEM] + [VMEM] * (3 + 2 * len(parts) + 3 * len(pieces)),
        out_specs=[HBM] * 3,
        out_shape=[shape] * 3,
        scratch_shapes=[pltpu.VMEM(k.shape, BF16)] * 3
        + [pltpu.SemaphoreType.DMA((3, (sum(parts) + 1) // 2))],
        compiler_params=pltpu.CompilerParams(vmem_limit_bytes=16 << 20),
        name="final",
    )(core, k, v, g, *mine, *other, *[x for piece in local for x in piece])


def after(values, *events):
    values = tuple(values)
    return lax.optimization_barrier(values + tuple(events))[: len(values)]


def hop(value, chips, a, b):
    sends = {2 * a: 2 * b, 2 * (chips - 1 - a) + 1: 2 * (chips - 1 - b) + 1}
    pairs = list(sends.items())
    for c in range(chips):
        free = [d for d in (2 * c, 2 * c + 1) if d not in sends]
        open_ = [d for d in (2 * c, 2 * c + 1) if d not in sends.values()]
        pairs += zip(free, open_)
    return lax.ppermute(value, ("seq", "sub"), pairs)


def swap(value):
    return lax.ppermute(value, "sub", [(0, 1), (1, 0)])


def body(*args):
    chips = lax.axis_size("seq")
    core, chip = lax.axis_index("sub").astype(jnp.int32), lax.axis_index("seq")
    rank = jnp.where(core == 0, chip, chips - 1 - chip)
    heads = args[0].shape[1] // DH
    chunks = min(CHUNKS, heads)
    parts = tuple(heads * (c + 1) // chunks - heads * c // chunks for c in range(chunks))
    core = core.reshape(1)
    arrives = [rank == step for step in range(chips)]
    core, *rest = lax.optimization_barrier((core, *arrives, *args))
    arrives, args = rest[:chips], rest[chips:]
    args, give, keep = states(core, parts, *args)
    total = [x + swap(y) for x, y in zip(keep, give)]
    mine = [jnp.zeros_like(x) for x in total]
    arrived = [hop(x, chips, 0, 1) for x in total]
    slots = (chips - 2) * chunks
    plan = PLAN if (heads, slots) == (sum(PLAN), len(PLAN)) else (0,) * (slots - 1) + (heads,)
    local, pieces = [], []
    event = total[-1]
    for step in range(1, chips - 1):
        for c in range(chunks):
            (arrived[c],) = after(arrived[c : c + 1], event)
            mine[c] = jnp.where(arrives[step], arrived[c], mine[c])
            sent = total[c] + arrived[c]
            arrived[c] = hop(sent, chips, step, step + 1)
            event = sent
            now = plan[(step - 1) * chunks + c]
            if now:
                local.append(intra(sum(pieces), now, *after(args, sent)))
                pieces.append(now)
                event = local[-1][0]
    other = []
    for c in range(chunks):
        (arrived[c],) = after(arrived[c : c + 1], event)
        mine[c] = jnp.where(arrives[chips - 1], arrived[c], mine[c])
        event = mine[c] + keep[c]
        other.append(swap(event))
    q, k, v, g = args
    return tuple(final(core, parts, tuple(pieces), k, v, g, mine, other, local))


def solution(mesh):
    placed = P(("rep", "seq", "sub"), "head")
    return jax.shard_map(
        body, mesh=mesh, in_specs=(placed,) * 4, out_specs=(placed,) * 3, check_vma=False
    )
```

```python
import functools

import jax
import jax.numpy as jnp
from jax import lax
from jax.experimental import pallas as pl
from jax.experimental.pallas import tpu as pltpu
from jax.sharding import PartitionSpec as P

DH = 128
F32 = jnp.float32
BF16 = jnp.bfloat16
VMEM = pl.BlockSpec(memory_space=pltpu.VMEM)
HBM = pl.BlockSpec(memory_space=pltpu.HBM)
SMEM = pl.BlockSpec(memory_space=pltpu.SMEM)


def product(left, right, left_axis, right_axis):
    return lax.dot_general(
        left, right, (((left_axis,), (right_axis,)), ((), ())), preferred_element_type=F32
    )


def head_columns(head):
    return slice(head * DH, (head + 1) * DH)


def states_kernel(core, q_hbm, k_hbm, v_hbm, g_hbm, q, k, v, g, *rest):
    parts = (len(rest) - 1) // 2
    give, keep, sems = rest[:parts], rest[parts : 2 * parts], rest[-1]
    copies = [
        pltpu.make_async_copy(source, target, sems.at[i])
        for i, (source, target) in enumerate(zip((q_hbm, k_hbm, v_hbm, g_hbm), (q, k, v, g)))
    ]
    for c in (0, 3, 1, 2):
        copies[c].start()
    is_first = core[0] == 0

    def state(left, right, outs):
        h = 0
        for out in outs:
            for i in range(out.shape[0]):
                c = head_columns(h)
                out[i] = product(left[:, c], right[:, c], 0, 0)
                h += 1

    for left, right, give_first in ((0, 3, True), (1, 2, False)):
        copies[left].wait()
        copies[right].wait()
        pair = (q, k, v, g)[left], (q, k, v, g)[right]

        @pl.when(is_first)
        def _():
            state(*pair, give if give_first else keep)

        @pl.when(jnp.logical_not(is_first))
        def _():
            state(*pair, keep if give_first else give)


def states(core, parts, q, k, v, g):
    outs = [pltpu.VMEM((n, DH, DH), F32) for n in parts] * 2
    result = pl.pallas_call(
        states_kernel,
        in_specs=[SMEM] + [HBM] * 4,
        out_specs=[VMEM] * (4 + len(outs)),
        out_shape=[pltpu.VMEM(q.shape, BF16)] * 4 + outs,
        scratch_shapes=[pltpu.SemaphoreType.DMA((4,))],
        compiler_params=pltpu.CompilerParams(vmem_limit_bytes=8 << 20),
        name="states",
    )(core, *[pltpu.with_memory_space_constraint(x, pltpu.HBM) for x in (q, k, v, g)])
    return result[:4], result[4 : 4 + len(parts)], result[4 + len(parts) :]


def intra_kernel(first, q, k, v, g, dq, dk, dv):
    rows = q.shape[0]
    row = lax.broadcasted_iota(jnp.int32, (rows, rows), 0)
    col = lax.broadcasted_iota(jnp.int32, (rows, rows), 1)
    for h in range(dq.shape[1] // DH):
        c, o = head_columns(first + h), head_columns(h)
        qh, kh, vh, gh = q[:, c], k[:, c], v[:, c], g[:, c]
        grad_scores = jnp.where(row >= col, product(gh, vh, 1, 1), 0.0).astype(BF16)
        dq[:, o] = product(grad_scores, kh, 1, 0)
        dk[:, o] = product(grad_scores, qh, 0, 0)
        attn_scores = jnp.where(row <= col, product(kh, qh, 1, 1), 0.0).astype(BF16)
        dv[:, o] = product(attn_scores, gh, 1, 0)


def intra(first, heads, q, k, v, g):
    return pl.pallas_call(
        functools.partial(intra_kernel, first),
        in_specs=[VMEM] * 4,
        out_specs=[VMEM] * 3,
        out_shape=[pltpu.VMEM((q.shape[0], heads * DH), F32)] * 3,
        compiler_params=pltpu.CompilerParams(vmem_limit_bytes=16 << 20),
        name="intra",
    )(q, k, v, g)


def final_kernel(parts, pieces, core, k, v, g, *rest):
    count = len(parts)
    mine, other, rest = rest[:count], rest[count : 2 * count], rest[2 * count :]
    local, rest = rest[: 3 * len(pieces)], rest[3 * len(pieces) :]
    (targets, outs, sems) = rest[:3], rest[3:6], rest[6]
    is_first = core[0] == 0
    of_part = [(p, i) for p, n in enumerate(parts) for i in range(n)]
    of_piece = [(p, i) for p, n in enumerate(pieces) for i in range(n)]
    heads = len(of_part)
    copies = []
    for h in range(heads):
        (part, i), (piece, j) = of_part[h], of_piece[h]
        c, o = head_columns(h), head_columns(j)
        prefix = jnp.where(is_first, mine[part][i], other[part][i]).astype(BF16)
        suffix = jnp.where(is_first, other[part][i], mine[part][i]).astype(BF16)
        local_q, local_k, local_v = (x[:, o] for x in local[3 * piece : 3 * piece + 3])
        outs[0][:, c] = (local_q + product(g[:, c], prefix, 1, 1)).astype(BF16)
        outs[1][:, c] = (local_k + product(v[:, c], suffix, 1, 1)).astype(BF16)
        outs[2][:, c] = (local_v + product(k[:, c], suffix, 1, 0)).astype(BF16)
        if h % 2 == 1 or h == heads - 1:
            cc = slice((h - h % 2) * DH, (h + 1) * DH)
            for n in range(3):
                copy = pltpu.make_async_copy(
                    outs[n].at[:, cc], targets[n].at[:, cc], sems.at[n, h // 2]
                )
                copy.start()
                copies.append(copy)
    for copy in copies:
        copy.wait()


def final(core, parts, pieces, k, v, g, mine, other, local):
    shape = jax.ShapeDtypeStruct(k.shape, BF16)
    return pl.pallas_call(
        functools.partial(final_kernel, parts, pieces),
        in_specs=[SMEM] + [VMEM] * (3 + 2 * len(parts) + 3 * len(pieces)),
        out_specs=[HBM] * 3,
        out_shape=[shape] * 3,
        scratch_shapes=[pltpu.VMEM(k.shape, BF16)] * 3
        + [pltpu.SemaphoreType.DMA((3, (sum(parts) + 1) // 2))],
        compiler_params=pltpu.CompilerParams(vmem_limit_bytes=16 << 20),
        name="final",
    )(core, k, v, g, *mine, *other, *[x for piece in local for x in piece])


def after(values, *events):
    values = tuple(values)
    return lax.optimization_barrier(values + tuple(events))[: len(values)]


def move(value, chips, hops):
    sends = {}
    for a, b in hops:
        sends[2 * a] = 2 * b
        sends[2 * (chips - 1 - a) + 1] = 2 * (chips - 1 - b) + 1
    pairs = list(sends.items())
    for c in range(chips):
        free = [d for d in (2 * c, 2 * c + 1) if d not in sends]
        open_ = [d for d in (2 * c, 2 * c + 1) if d not in sends.values()]
        pairs += zip(free, open_, strict=True)
    return lax.ppermute(value, ("seq", "sub"), pairs)


def step_hops(chips, step):
    return [(step, step + 1), (chips - 2 - step, chips - 1 - step)]


def swap(value):
    return lax.ppermute(value, "sub", [(0, 1), (1, 0)])


def body(*args):
    chips = lax.axis_size("seq")
    last = chips - 1
    core, chip = lax.axis_index("sub").astype(jnp.int32), lax.axis_index("seq")
    rank = jnp.where(core == 0, chip, last - chip)
    heads = args[0].shape[1] // DH
    parts = (heads // 2, heads - heads // 2)
    pieces = parts
    core = core.reshape(1)
    at = [rank == r for r in range(chips)] + [(rank == 1) | (rank == 3)]
    core, *rest = lax.optimization_barrier((core, *at, *args))
    at, args = rest[: chips + 1], rest[chips + 1 :]
    args, give, keep = states(core, parts, *args)
    total_a, total_b = (x + swap(y) for x, y in zip(keep, give))
    zero_a, zero_b = jnp.zeros_like(total_a), jnp.zeros_like(total_b)
    arrived_a, arrived_b = (move(x, chips, step_hops(chips, 0)) for x in (total_a, total_b))
    local_a = intra(0, parts[0], *after(args, total_a, total_b))
    (arrived_a,) = after((arrived_a,), local_a[0])
    mine_a = jnp.where(at[1], arrived_a, zero_a)
    direct = chips == 4
    mine_b = jnp.where(at[-1] if direct else at[1], arrived_b, zero_b)
    for step in range(1, last):
        sent_a = total_a + arrived_a
        arrived_a = move(sent_a, chips, step_hops(chips, step))
        if not (direct and step == last - 1):
            (arrived_b,) = after((arrived_b,), sent_a)
            sent_b = total_b + arrived_b
            arrived_b = move(sent_b, chips, step_hops(chips, step))
            if direct:
                far_b = move(sent_b, chips, [(1, 3), (0, 1)])
        if step == last - 1:
            local_b = intra(parts[0], parts[1], *after(args, sent_a))
            if direct:
                arrived_a, far_b = after((arrived_a, far_b), local_b[0])
                mine_b = mine_b + jnp.where(at[3], far_b, zero_b)
                mine_b = jnp.where(at[2], arrived_b, mine_b)
            else:
                (arrived_a,) = after((arrived_a,), local_b[0])
        if not direct:
            mine_b = jnp.where(at[step + 1], arrived_b, mine_b)
        mine_a = jnp.where(at[step + 1], arrived_a, mine_a)
    other_b = swap(mine_b + keep[1])
    other_a = swap(mine_a + keep[0])
    q, k, v, g = args
    return tuple(
        final(
            core, parts, pieces, k, v, g, (mine_a, mine_b), (other_a, other_b), (local_a, local_b)
        )
    )


def solution(mesh):
    placed = P(("rep", "seq", "sub"), "head")
    return jax.shard_map(
        body, mesh=mesh, in_specs=(placed,) * 4, out_specs=(placed,) * 3, check_vma=False
    )
```

```python
import functools

import jax
import jax.numpy as jnp
from jax import lax
from jax.experimental import pallas as pl
from jax.experimental.pallas import tpu as pltpu
from jax.sharding import PartitionSpec as P

DH = 128
CHUNKS = 2
PLAN = (2, 1, 3, 1, 1)
F32 = jnp.float32
BF16 = jnp.bfloat16
VMEM = pl.BlockSpec(memory_space=pltpu.VMEM)
HBM = pl.BlockSpec(memory_space=pltpu.HBM)
SMEM = pl.BlockSpec(memory_space=pltpu.SMEM)


def product(left, right, left_axis, right_axis):
    return lax.dot_general(
        left, right, (((left_axis,), (right_axis,)), ((), ())), preferred_element_type=F32
    )


def head_columns(head):
    return slice(head * DH, (head + 1) * DH)


def states_kernel(aliased, place, q_hbm, k_hbm, v_hbm, g_hbm, *rest):
    rest = rest[aliased:]
    q, k, v, g = rest[:4]
    parts = (len(rest) - 5) // 2
    keep, give, sems = rest[4 : 4 + parts], rest[4 + parts : 4 + 2 * parts], rest[-1]
    copies = [
        pltpu.make_async_copy(source, target, sems.at[i])
        for i, (source, target) in enumerate(zip((q_hbm, k_hbm, v_hbm, g_hbm), (q, k, v, g)))
    ]
    is_first = place[0] == 0

    def state(left, right, outs):
        h = 0
        for out in outs:
            for i in range(out.shape[0]):
                c = head_columns(h)
                out[i] = product(left[:, c], right[:, c], 0, 0)
                h += 1

    @pl.when(place[1] == 1)
    def _():
        for c in (0, 3, 1, 2):
            copies[c].start()
        for left, right, give_first in ((0, 3, True), (1, 2, False)):
            copies[left].wait()
            copies[right].wait()
            pair = (q, k, v, g)[left], (q, k, v, g)[right]

            @pl.when(is_first)
            def _():
                state(*pair, give if give_first else keep)

            @pl.when(jnp.logical_not(is_first))
            def _():
                state(*pair, keep if give_first else give)


def states(place, parts, args, filled=()):
    outs = [pltpu.VMEM((n, DH, DH), F32) for n in parts]
    result = pl.pallas_call(
        functools.partial(states_kernel, len(filled)),
        in_specs=[SMEM] + [HBM] * 4 + [VMEM] * len(filled),
        out_specs=[VMEM] * (4 + 2 * len(outs)),
        out_shape=[pltpu.VMEM(args[0].shape, BF16)] * 4 + outs + outs,
        scratch_shapes=[pltpu.SemaphoreType.DMA((4,))],
        input_output_aliases={5 + i: i for i in range(len(filled))},
        compiler_params=pltpu.CompilerParams(vmem_limit_bytes=8 << 20),
        name="states",
    )(place, *[pltpu.with_memory_space_constraint(x, pltpu.HBM) for x in args], *filled)
    return result[: 4 + len(parts)], result[4 + len(parts) :]


def intra_kernel(first, q, k, v, g, dq, dk, dv):
    rows = q.shape[0]
    row = lax.broadcasted_iota(jnp.int32, (rows, rows), 0)
    col = lax.broadcasted_iota(jnp.int32, (rows, rows), 1)
    for h in range(dq.shape[1] // DH):
        c, o = head_columns(first + h), head_columns(h)
        qh, kh, vh, gh = q[:, c], k[:, c], v[:, c], g[:, c]
        grad_scores = jnp.where(row >= col, product(gh, vh, 1, 1), 0.0).astype(BF16)
        dq[:, o] = product(grad_scores, kh, 1, 0)
        dk[:, o] = product(grad_scores, qh, 0, 0)
        attn_scores = jnp.where(row <= col, product(kh, qh, 1, 1), 0.0).astype(BF16)
        dv[:, o] = product(attn_scores, gh, 1, 0)


def intra(first, heads, q, k, v, g):
    return pl.pallas_call(
        functools.partial(intra_kernel, first),
        in_specs=[VMEM] * 4,
        out_specs=[VMEM] * 3,
        out_shape=[pltpu.VMEM((q.shape[0], heads * DH), F32)] * 3,
        compiler_params=pltpu.CompilerParams(vmem_limit_bytes=16 << 20),
        name="intra",
    )(q, k, v, g)


def final_kernel(parts, pieces, core, k, v, g, *rest):
    count = len(parts)
    mine, other, rest = rest[:count], rest[count : 2 * count], rest[2 * count :]
    local, rest = rest[: 3 * len(pieces)], rest[3 * len(pieces) :]
    (targets, outs, sems) = rest[:3], rest[3:6], rest[6]
    is_first = core[0] == 0
    of_part = [(p, i) for p, n in enumerate(parts) for i in range(n)]
    of_piece = [(p, i) for p, n in enumerate(pieces) for i in range(n)]
    heads = len(of_part)
    copies = []
    for h in range(heads):
        (part, i), (piece, j) = of_part[h], of_piece[h]
        c, o = head_columns(h), head_columns(j)
        prefix = jnp.where(is_first, mine[part][i], other[part][i]).astype(BF16)
        suffix = jnp.where(is_first, other[part][i], mine[part][i]).astype(BF16)
        local_q, local_k, local_v = (x[:, o] for x in local[3 * piece : 3 * piece + 3])
        outs[0][:, c] = (local_q + product(g[:, c], prefix, 1, 1)).astype(BF16)
        outs[1][:, c] = (local_k + product(v[:, c], suffix, 1, 1)).astype(BF16)
        outs[2][:, c] = (local_v + product(k[:, c], suffix, 1, 0)).astype(BF16)
        if h % 2 == 1 or h == heads - 1:
            cc = slice((h - h % 2) * DH, (h + 1) * DH)
            for n in range(3):
                copy = pltpu.make_async_copy(
                    outs[n].at[:, cc], targets[n].at[:, cc], sems.at[n, h // 2]
                )
                copy.start()
                copies.append(copy)
    for copy in copies:
        copy.wait()


def final(core, parts, pieces, k, v, g, mine, other, local):
    shape = jax.ShapeDtypeStruct(k.shape, BF16)
    return pl.pallas_call(
        functools.partial(final_kernel, parts, pieces),
        in_specs=[SMEM] + [VMEM] * (3 + 2 * len(parts) + 3 * len(pieces)),
        out_specs=[HBM] * 3,
        out_shape=[shape] * 3,
        scratch_shapes=[pltpu.VMEM(k.shape, BF16)] * 3
        + [pltpu.SemaphoreType.DMA((3, (sum(parts) + 1) // 2))],
        compiler_params=pltpu.CompilerParams(vmem_limit_bytes=16 << 20),
        name="final",
    )(core, k, v, g, *mine, *other, *[x for piece in local for x in piece])


def after(values, *events):
    values = tuple(values)
    return lax.optimization_barrier(values + tuple(events))[: len(values)]


def move(value, chips, hops):
    pairs = []
    for a, b in hops:
        pairs += [(2 * a, 2 * b), (2 * (chips - 1 - a) + 1, 2 * (chips - 1 - b) + 1)]
    return lax.ppermute(value, ("seq", "sub"), pairs)


def swap(value):
    return lax.ppermute(value, "sub", [(0, 1), (1, 0)])


def body(*args):
    chips = lax.axis_size("seq")
    last = chips - 1
    core, chip = lax.axis_index("sub").astype(jnp.int32), lax.axis_index("seq")
    at_end = jnp.logical_or(chip == 0, chip == last)
    heads = args[0].shape[1] // DH
    chunks = CHUNKS
    parts = tuple(heads * (c + 1) // chunks - heads * c // chunks for c in range(chunks))
    slots = 1 + (chips - 2) * chunks
    plan = PLAN if (heads, slots) == (sum(PLAN), len(PLAN)) else (0,) * (slots - 1) + (heads,)
    at_end_now = jnp.stack([core, at_end.astype(jnp.int32)])
    elsewhere = jnp.stack([core, 1 - at_end.astype(jnp.int32)])
    core = core.reshape(1)
    at_end, at_end_now, elsewhere, core, *args = lax.optimization_barrier(
        (at_end, at_end_now, elsewhere, core, *args)
    )

    filled, give = states(at_end_now, parts, args)
    early = [swap(x) for x in give]
    first = [x + y for x, y in zip(filled[4:], early)]
    arrived = [move(x, chips, [(0, 1)]) for x in first]
    filled, give = states(elsewhere, parts, args, after(filled, *first))
    args, keep = filled[:4], filled[4:]
    late = [swap(x) for x in give]

    local, pieces = [], []

    def local_piece(count, event):
        if count:
            local.append(intra(sum(pieces), count, *after(args, event)))
            pieces.append(count)
            event = local[-1][0]
        return event

    event = local_piece(plan[0], give[-1])
    mine = [None] * chunks
    total = [None] * chunks
    for step in range(1, last):
        for c in range(chunks):
            (arrived[c],) = after(arrived[c : c + 1], event)
            mine[c] = arrived[c] if mine[c] is None else mine[c] + arrived[c]
            if step == 1:
                sent = keep[c] + arrived[c]
                (late[c],) = after(late[c : c + 1], sent)
                other = jnp.where(at_end, early[c], late[c])
                total[c] = keep[c] + other
                sent = sent + other
            else:
                sent = total[c] + arrived[c]
            arrived[c] = move(sent, chips, [(step, step + 1)])
            event = local_piece(plan[1 + (step - 1) * chunks + c], sent)
    other = []
    for c in range(chunks):
        (arrived[c],) = after(arrived[c : c + 1], event)
        mine[c] = mine[c] + arrived[c]
        event = mine[c] + keep[c]
        other.append(swap(event))
    q, k, v, g = args
    return tuple(final(core, parts, tuple(pieces), k, v, g, mine, other, local))


def solution(mesh):
    placed = P(("rep", "seq", "sub"), "head")
    return jax.shard_map(
        body, mesh=mesh, in_specs=(placed,) * 4, out_specs=(placed,) * 3, check_vma=False
    )
```

```python
import functools

import jax
import jax.numpy as jnp
from jax import lax
from jax.experimental import pallas as pl
from jax.experimental.pallas import tpu as pltpu
from jax.sharding import PartitionSpec as P

DH = 128
CHUNKS = 4
PLAN = (3, 0, 0, 0, 0, 1, 1, 1, 2)
F32 = jnp.float32
BF16 = jnp.bfloat16
VMEM = pl.BlockSpec(memory_space=pltpu.VMEM)
HBM = pl.BlockSpec(memory_space=pltpu.HBM)
SMEM = pl.BlockSpec(memory_space=pltpu.SMEM)


def product(left, right, left_axis, right_axis):
    return lax.dot_general(
        left, right, (((left_axis,), (right_axis,)), ((), ())), preferred_element_type=F32
    )


def head_columns(head):
    return slice(head * DH, (head + 1) * DH)


def states_kernel(core, q_hbm, k_hbm, v_hbm, g_hbm, q, k, v, g, *rest):
    chunks = (len(rest) - 1) // 2
    keep, give, sems = rest[:chunks], rest[chunks : 2 * chunks], rest[-1]
    copies = [
        pltpu.make_async_copy(source, target, sems.at[i])
        for i, (source, target) in enumerate(zip((q_hbm, k_hbm, v_hbm, g_hbm), (q, k, v, g)))
    ]
    for c in (1, 2, 0, 3):
        copies[c].start()
    half = q.shape[1] // 2
    for left, right, place in ((1, 2, 0), (0, 3, 1)):
        copies[left].wait()
        copies[right].wait()
        x, y = (q, k, v, g)[left], (q, k, v, g)[right]
        for outs, start in ((give, (1 - core[0]) * half), (keep, core[0] * half)):
            h = 0
            for out in outs:
                count = out.shape[0] // 2
                for i in range(count):
                    c = pl.ds(pl.multiple_of(start + h * DH, DH), DH)
                    out[place * count + i] = product(x[:, c], y[:, c], 0, 0)
                    h += 1


def states(core, parts, q, k, v, g):
    outs = [pltpu.VMEM((2 * n, DH, DH), F32) for n in parts] * 2
    result = pl.pallas_call(
        states_kernel,
        in_specs=[SMEM] + [HBM] * 4,
        out_specs=[VMEM] * (4 + len(outs)),
        out_shape=[pltpu.VMEM(q.shape, BF16)] * 4 + outs,
        scratch_shapes=[pltpu.SemaphoreType.DMA((4,))],
        compiler_params=pltpu.CompilerParams(vmem_limit_bytes=8 << 20),
        name="states",
    )(core, *[pltpu.with_memory_space_constraint(x, pltpu.HBM) for x in (q, k, v, g)])
    return result[:4], result[4 : 4 + len(parts)], result[4 + len(parts) :]


def intra_kernel(first, q, k, v, g, dq, dk, dv):
    rows = q.shape[0]
    row = lax.broadcasted_iota(jnp.int32, (rows, rows), 0)
    col = lax.broadcasted_iota(jnp.int32, (rows, rows), 1)
    for h in range(dq.shape[1] // DH):
        c, o = head_columns(first + h), head_columns(h)
        qh, kh, vh, gh = q[:, c], k[:, c], v[:, c], g[:, c]
        grad_scores = jnp.where(row >= col, product(gh, vh, 1, 1), 0.0).astype(BF16)
        dq[:, o] = product(grad_scores, kh, 1, 0)
        dk[:, o] = product(grad_scores, qh, 0, 0)
        attn_scores = jnp.where(row <= col, product(kh, qh, 1, 1), 0.0).astype(BF16)
        dv[:, o] = product(attn_scores, gh, 1, 0)


def intra(first, heads, q, k, v, g):
    return pl.pallas_call(
        functools.partial(intra_kernel, first),
        in_specs=[VMEM] * 4,
        out_specs=[VMEM] * 3,
        out_shape=[pltpu.VMEM((q.shape[0], heads * DH), F32)] * 3,
        compiler_params=pltpu.CompilerParams(vmem_limit_bytes=16 << 20),
        name="intra",
    )(q, k, v, g)


def final_kernel(parts, pieces, core, k, v, g, *rest):
    count = len(parts)
    own, other, rest = rest[:count], rest[count : 2 * count], rest[2 * count :]
    local, rest = rest[: 3 * len(pieces)], rest[3 * len(pieces) :]
    (targets, outs, sems) = rest[:3], rest[3:6], rest[6]
    of_part = [(half, p, i) for half in (0, 1) for p, n in enumerate(parts) for i in range(n)]
    of_piece = [(p, i) for p, n in enumerate(pieces) for i in range(n)]
    heads = len(of_part)
    copies = []
    for h in range(heads):
        (half, part, i), (piece, j) = of_part[h], of_piece[h]
        c, o = head_columns(h), head_columns(j)
        mine = core[0] == half
        prefix, suffix = (
            jnp.where(mine, own[part][n], other[part][n]).astype(BF16)
            for n in (i, parts[part] + i)
        )
        local_q, local_k, local_v = (x[:, o] for x in local[3 * piece : 3 * piece + 3])
        outs[0][:, c] = (local_q + product(g[:, c], prefix, 1, 1)).astype(BF16)
        outs[1][:, c] = (local_k + product(v[:, c], suffix, 1, 1)).astype(BF16)
        outs[2][:, c] = (local_v + product(k[:, c], suffix, 1, 0)).astype(BF16)
        if h % 2 == 1 or h == heads - 1:
            cc = slice((h - h % 2) * DH, (h + 1) * DH)
            for n in range(3):
                copy = pltpu.make_async_copy(
                    outs[n].at[:, cc], targets[n].at[:, cc], sems.at[n, h // 2]
                )
                copy.start()
                copies.append(copy)
    for copy in copies:
        copy.wait()


def final(core, parts, pieces, k, v, g, own, other, local):
    shape = jax.ShapeDtypeStruct(k.shape, BF16)
    return pl.pallas_call(
        functools.partial(final_kernel, parts, pieces),
        in_specs=[SMEM] + [VMEM] * (3 + 2 * len(parts) + 3 * len(pieces)),
        out_specs=[HBM] * 3,
        out_shape=[shape] * 3,
        scratch_shapes=[pltpu.VMEM(k.shape, BF16)] * 3
        + [pltpu.SemaphoreType.DMA((3, (2 * sum(parts) + 1) // 2))],
        compiler_params=pltpu.CompilerParams(vmem_limit_bytes=16 << 20),
        name="final",
    )(core, k, v, g, *own, *other, *[x for piece in local for x in piece])


def after(values, *events):
    values = tuple(values)
    return lax.optimization_barrier(values + tuple(events))[: len(values)]


def swap(value):
    return lax.ppermute(value, "sub", [(0, 1), (1, 0)])


def exchange(value, chips, step):
    partner = {}
    for low in (step, chips - 2 - step):
        for core in (0, 1):
            a, b = 2 * low + core, 2 * low + 2 + core
            partner[a], partner[b] = b, a
    pairs = [(d, partner.get(d, d ^ 1)) for d in range(2 * chips)]
    return lax.ppermute(value, ("seq", "sub"), pairs)


def body(*args):
    chips = lax.axis_size("seq")
    core, chip = lax.axis_index("sub").astype(jnp.int32), lax.axis_index("seq")
    heads = args[0].shape[1] // DH
    chunks = min(CHUNKS, heads // 2)
    parts = tuple(
        heads // 2 * (c + 1) // chunks - heads // 2 * c // chunks for c in range(chunks)
    )
    slots = 1 + (chips - 2) * chunks
    plan = PLAN if (heads, slots) == (sum(PLAN), len(PLAN)) else (0,) * (slots - 1) + (heads,)
    at = [chip == c for c in range(chips)]
    core, first_core, *rest = lax.optimization_barrier((core.reshape(1), core == 0, *at, *args))
    at, args = rest[:chips], rest[chips:]
    args, keep, give = states(core, parts, *args)
    got = [swap(x) for x in give]
    total = [None] * chunks
    local, pieces = [], []

    def local_piece(count, event):
        if count:
            local.append(intra(sum(pieces), count, *after(args, event)))
            pieces.append(count)
            event = local[-1][0]
        return event

    prefix = [jnp.zeros_like(x[:n]) for x, n in zip(keep, parts)]
    suffix = list(prefix)
    arrived = [None] * chunks
    event = None
    for step in range(chips):
        if step == 1:
            event = local_piece(plan[0], event)
        for c, n in enumerate(parts):
            if step == 0:
                if c:
                    (got[c],) = after(got[c : c + 1], event)
                total[c] = keep[c] + got[c]
            else:
                (arrived[c],) = after(arrived[c : c + 1], event)
                prefix[c] = jnp.where(at[step], arrived[c], prefix[c])
                suffix[c] = jnp.where(at[chips - 1 - step], arrived[c], suffix[c])
            if step == chips - 1:
                event = prefix[c]
                continue
            sent = jnp.where(at[step], total[c][:n], total[c][n:])
            if step:
                sent = sent + arrived[c]
            arrived[c] = exchange(sent, chips, step)
            event = sent
            if step:
                event = local_piece(plan[1 + (step - 1) * chunks + c], sent)
    own, other = [], []
    for c, n in enumerate(parts):
        zero = jnp.zeros_like(prefix[c])
        own.append(
            jnp.concatenate(
                [
                    prefix[c] + jnp.where(first_core, zero, got[c][:n]),
                    suffix[c] + jnp.where(first_core, got[c][n:], zero),
                ]
            )
        )
        other.append(
            swap(
                jnp.concatenate(
                    [
                        prefix[c] + jnp.where(first_core, keep[c][:n], zero),
                        suffix[c] + jnp.where(first_core, zero, keep[c][n:]),
                    ]
                )
            )
        )
    q, k, v, g = args
    return tuple(final(core, parts, tuple(pieces), k, v, g, own, other, local))


def solution(mesh):
    placed = P(("rep", "seq", "sub"), "head")
    return jax.shard_map(
        body, mesh=mesh, in_specs=(placed,) * 4, out_specs=(placed,) * 3, check_vma=False
    )
```

```python
import functools

import jax
import jax.numpy as jnp
from jax import lax
from jax.experimental import pallas as pl
from jax.experimental.pallas import tpu as pltpu
from jax.sharding import PartitionSpec as P

DH = 128
CHUNKS = 2
PLAN = (5, 1, 2, 0, 0)
F32 = jnp.float32
BF16 = jnp.bfloat16
VMEM = pl.BlockSpec(memory_space=pltpu.VMEM)
HBM = pl.BlockSpec(memory_space=pltpu.HBM)
SMEM = pl.BlockSpec(memory_space=pltpu.SMEM)


def product(left, right, left_axis, right_axis):
    return lax.dot_general(
        left, right, (((left_axis,), (right_axis,)), ((), ())), preferred_element_type=F32
    )


def head_columns(head):
    return slice(head * DH, (head + 1) * DH)


def states_kernel(core, q_hbm, k_hbm, v_hbm, g_hbm, q, k, v, g, *rest):
    chunks = (len(rest) - 1) // 2
    keep, give, sems = rest[:chunks], rest[chunks : 2 * chunks], rest[-1]
    copies = [
        pltpu.make_async_copy(source, target, sems.at[i])
        for i, (source, target) in enumerate(zip((q_hbm, k_hbm, v_hbm, g_hbm), (q, k, v, g)))
    ]
    for c in (1, 2, 0, 3):
        copies[c].start()
    half = q.shape[1] // 2
    for left, right, place in ((1, 2, 0), (0, 3, 1)):
        copies[left].wait()
        copies[right].wait()
        x, y = (q, k, v, g)[left], (q, k, v, g)[right]
        for outs, start in ((give, (1 - core[0]) * half), (keep, core[0] * half)):
            h = 0
            for out in outs:
                count = out.shape[0] // 2
                for i in range(count):
                    c = pl.ds(pl.multiple_of(start + h * DH, DH), DH)
                    out[place * count + i] = product(x[:, c], y[:, c], 0, 0)
                    h += 1


def states(core, parts, q, k, v, g):
    outs = [pltpu.VMEM((2 * n, DH, DH), F32) for n in parts] * 2
    result = pl.pallas_call(
        states_kernel,
        in_specs=[SMEM] + [HBM] * 4,
        out_specs=[VMEM] * (4 + len(outs)),
        out_shape=[pltpu.VMEM(q.shape, BF16)] * 4 + outs,
        scratch_shapes=[pltpu.SemaphoreType.DMA((4,))],
        compiler_params=pltpu.CompilerParams(vmem_limit_bytes=8 << 20),
        name="states",
    )(core, *[pltpu.with_memory_space_constraint(x, pltpu.HBM) for x in (q, k, v, g)])
    return result[:4], result[4 : 4 + len(parts)], result[4 + len(parts) :]


def intra_kernel(first, heads, q, k, v, g, *rest):
    dq, dk, dv = rest[-3:]
    rows = q.shape[0]
    row = lax.broadcasted_iota(jnp.int32, (rows, rows), 0)
    col = lax.broadcasted_iota(jnp.int32, (rows, rows), 1)
    for h in range(first, first + heads):
        c = head_columns(h)
        qh, kh, vh, gh = q[:, c], k[:, c], v[:, c], g[:, c]
        grad_scores = jnp.where(row >= col, product(gh, vh, 1, 1), 0.0).astype(BF16)
        dq[:, c] = product(grad_scores, kh, 1, 0)
        dk[:, c] = product(grad_scores, qh, 0, 0)
        attn_scores = jnp.where(row <= col, product(kh, qh, 1, 1), 0.0).astype(BF16)
        dv[:, c] = product(attn_scores, gh, 1, 0)


def intra(first, heads, q, k, v, g, filled):
    return pl.pallas_call(
        functools.partial(intra_kernel, first, heads),
        in_specs=[VMEM] * (4 + len(filled)),
        out_specs=[VMEM] * 3,
        out_shape=[pltpu.VMEM(q.shape, F32)] * 3,
        input_output_aliases={4 + i: i for i in range(len(filled))},
        compiler_params=pltpu.CompilerParams(vmem_limit_bytes=16 << 20),
        name="intra",
    )(q, k, v, g, *filled)


def final_kernel(groups, heads, aliased, core, k, v, g, dqi, dki, dvi, *rest):
    states, rest = rest[: len(groups)], rest[len(groups) + aliased :]
    (targets, outs, sems) = rest[:3], rest[3:6], rest[6]
    copies, done = [], 0
    for n, ((other, first, count), both) in enumerate(zip(groups, states)):
        half = 1 - core[0] if other else core[0]
        start = half * (heads // 2) + first
        for i in range(count):
            c, w = pl.ds(pl.multiple_of((start + i) * DH, DH), DH), head_columns(done + i)
            before, behind = both[i].astype(BF16), both[count + i].astype(BF16)
            outs[0][:, w] = (dqi[:, c] + product(g[:, c], before, 1, 1)).astype(BF16)
            outs[1][:, w] = (dki[:, c] + product(v[:, c], behind, 1, 1)).astype(BF16)
            outs[2][:, w] = (dvi[:, c] + product(k[:, c], behind, 1, 0)).astype(BF16)
        here = slice(done * DH, (done + count) * DH)
        there = pl.ds(pl.multiple_of(start * DH, DH), count * DH)
        for m in range(3):
            copy = pltpu.make_async_copy(
                outs[m].at[:, here], targets[m].at[:, there], sems.at[n, m]
            )
            copy.start()
            copies.append(copy)
        done += count
    for copy in copies:
        copy.wait()


def final(groups, core, args, local, states, filled):
    _, k, v, g = args
    shape = jax.ShapeDtypeStruct(k.shape, BF16)
    inputs = (core, k, v, g, *local, *states)
    width = sum(count for _, _, count in groups) * DH
    return pl.pallas_call(
        functools.partial(final_kernel, groups, k.shape[1] // DH, len(filled)),
        in_specs=[SMEM] + [VMEM] * (len(inputs) - 1) + [HBM] * len(filled),
        out_specs=[HBM] * 3,
        out_shape=[shape] * 3,
        scratch_shapes=[pltpu.VMEM((k.shape[0], width), BF16)] * 3
        + [pltpu.SemaphoreType.DMA((len(groups), 3))],
        input_output_aliases={len(inputs) + i: i for i in range(len(filled))},
        compiler_params=pltpu.CompilerParams(vmem_limit_bytes=8 << 20),
        name="final",
    )(*inputs, *filled)


def after(values, *events):
    values = tuple(values)
    return lax.optimization_barrier(values + tuple(events))[: len(values)]


def swap(value):
    return lax.ppermute(value, "sub", [(0, 1), (1, 0)])


def exchange(value, chips, step):
    partner = {}
    for low in (step, chips - 2 - step):
        for core in (0, 1):
            a, b = 2 * low + core, 2 * low + 2 + core
            partner[a], partner[b] = b, a
    pairs = [(d, partner.get(d, d ^ 1)) for d in range(2 * chips)]
    return lax.ppermute(value, ("seq", "sub"), pairs)


def body(*args):
    chips = lax.axis_size("seq")
    core, chip = lax.axis_index("sub").astype(jnp.int32), lax.axis_index("seq")
    heads = args[0].shape[1] // DH
    chunks = min(CHUNKS, heads // 2)
    parts = tuple(
        heads // 2 * (c + 1) // chunks - heads // 2 * c // chunks for c in range(chunks)
    )
    slots = 1 + (chips - 2) * chunks
    plan = PLAN if (heads, slots) == (sum(PLAN), len(PLAN)) else (0,) * (slots - 1) + (heads,)
    at = [chip == c for c in range(chips)]
    core, first_core, *rest = lax.optimization_barrier((core.reshape(1), core == 0, *at, *args))
    at, args = rest[:chips], rest[chips:]
    args, keep, give = states(core, parts, *args)
    got = [swap(x) for x in give]
    total = [None] * chunks
    local, done = (), 0

    def local_piece(count, event):
        nonlocal local, done
        if count:
            local = intra(done, count, *after(args, event), local)
            done += count
            event = local[0]
        return event

    prefix = [jnp.zeros_like(x[:n]) for x, n in zip(keep, parts)]
    suffix = list(prefix)
    arrived = [None] * chunks
    event, outs, own, other = None, (), [], []
    for step in range(chips):
        if step == 1:
            event = local_piece(plan[0], event)
        for c, n in enumerate(parts):
            if step == 0:
                if c:
                    (got[c],) = after(got[c : c + 1], event)
                total[c] = keep[c] + got[c]
            else:
                (arrived[c],) = after(arrived[c : c + 1], event)
                prefix[c] = jnp.where(at[step], arrived[c], prefix[c])
                suffix[c] = jnp.where(at[chips - 1 - step], arrived[c], suffix[c])
            if step == chips - 1:
                zero = jnp.zeros_like(prefix[c])
                own.append(
                    jnp.concatenate(
                        [
                            prefix[c] + jnp.where(first_core, zero, got[c][:n]),
                            suffix[c] + jnp.where(first_core, got[c][n:], zero),
                        ]
                    )
                )
                lend = jnp.concatenate(
                    [
                        prefix[c] + jnp.where(first_core, keep[c][:n], zero),
                        suffix[c] + jnp.where(first_core, zero, keep[c][n:]),
                    ]
                )
                other.append(swap(lend))
                groups, use = [(False, sum(parts[:c]), n)], [own[c]]
                if c:
                    groups.append((True, sum(parts[: c - 1]), parts[c - 1]))
                    use.append(other[c - 1])
                outs = final(tuple(groups), core, args, local, use, outs)
                event = outs[0]
                continue
            sent = jnp.where(at[step], total[c][:n], total[c][n:])
            if step:
                sent = sent + arrived[c]
            arrived[c] = exchange(sent, chips, step)
            event = sent
            if step:
                event = local_piece(plan[1 + (step - 1) * chunks + c], sent)
    last_group = (True, sum(parts[:-1]), parts[-1])
    return tuple(final((last_group,), core, args, local, other[-1:], outs))


def solution(mesh):
    placed = P(("rep", "seq", "sub"), "head")
    return jax.shard_map(
        body, mesh=mesh, in_specs=(placed,) * 4, out_specs=(placed,) * 3, check_vma=False
    )
```

```python
import functools

import jax
import jax.numpy as jnp
from jax import lax
from jax.experimental import pallas as pl
from jax.experimental.pallas import tpu as pltpu
from jax.sharding import PartitionSpec as P

DH = 128
CHUNKS = 2
PLAN = (5, 1, 2, 0, 0)
F32 = jnp.float32
BF16 = jnp.bfloat16
VMEM = pl.BlockSpec(memory_space=pltpu.VMEM)
HBM = pl.BlockSpec(memory_space=pltpu.HBM)
SMEM = pl.BlockSpec(memory_space=pltpu.SMEM)


def product(left, right, left_axis, right_axis):
    return lax.dot_general(
        left, right, (((left_axis,), (right_axis,)), ((), ())), preferred_element_type=F32
    )


def head_columns(head):
    return slice(head * DH, (head + 1) * DH)


def states_kernel(first, count, aliased, core, q_hbm, k_hbm, v_hbm, g_hbm, *rest):
    q, k, v, g, keep, give, sems = rest[aliased:]
    width = q.shape[1] // 2
    copies = []
    for source, target in ((k_hbm, k), (v_hbm, v), (q_hbm, q), (g_hbm, g)):
        for half in (0, 1):
            c = pl.ds(half * width + first * DH, count * DH)
            copy = pltpu.make_async_copy(source.at[:, c], target.at[:, c], sems.at[len(copies)])
            copy.start()
            copies.append(copy)
    for n, (x, y) in enumerate(((k, v), (q, g))):
        for copy in copies[4 * n : 4 * n + 4]:
            copy.wait()
        for out, half in ((give, 1 - core[0]), (keep, core[0])):
            for i in range(count):
                c = pl.ds(pl.multiple_of(half * width + (first + i) * DH, DH), DH)
                out[n * count + i] = product(x[:, c], y[:, c], 0, 0)


def states(core, first, count, args, filled):
    result = pl.pallas_call(
        functools.partial(states_kernel, first, count, len(filled)),
        in_specs=[SMEM] + [HBM] * 4 + [VMEM] * len(filled),
        out_specs=[VMEM] * 6,
        out_shape=[pltpu.VMEM(args[0].shape, BF16)] * 4
        + [pltpu.VMEM((2 * count, DH, DH), F32)] * 2,
        scratch_shapes=[pltpu.SemaphoreType.DMA((8,))],
        input_output_aliases={5 + i: i for i in range(len(filled))},
        compiler_params=pltpu.CompilerParams(vmem_limit_bytes=8 << 20),
        name="states",
    )(core, *[pltpu.with_memory_space_constraint(x, pltpu.HBM) for x in args], *filled)
    return result[:4], *result[4:]


def intra_kernel(first, heads, q, k, v, g, *rest):
    dq, dk, dv = rest[-3:]
    rows = q.shape[0]
    row = lax.broadcasted_iota(jnp.int32, (rows, rows), 0)
    col = lax.broadcasted_iota(jnp.int32, (rows, rows), 1)
    for h in range(first, first + heads):
        c = head_columns(h)
        qh, kh, vh, gh = q[:, c], k[:, c], v[:, c], g[:, c]
        grad_scores = jnp.where(row >= col, product(gh, vh, 1, 1), 0.0).astype(BF16)
        dq[:, c] = product(grad_scores, kh, 1, 0)
        dk[:, c] = product(grad_scores, qh, 0, 0)
        attn_scores = jnp.where(row <= col, product(kh, qh, 1, 1), 0.0).astype(BF16)
        dv[:, c] = product(attn_scores, gh, 1, 0)


def intra(first, heads, q, k, v, g, filled):
    return pl.pallas_call(
        functools.partial(intra_kernel, first, heads),
        in_specs=[VMEM] * (4 + len(filled)),
        out_specs=[VMEM] * 3,
        out_shape=[pltpu.VMEM(q.shape, F32)] * 3,
        input_output_aliases={4 + i: i for i in range(len(filled))},
        compiler_params=pltpu.CompilerParams(vmem_limit_bytes=16 << 20),
        name="intra",
    )(q, k, v, g, *filled)


def final_kernel(groups, send, core, k, v, g, dqi, dki, dvi, *rest):
    count_new = len(groups)
    states, rest = rest[:count_new], rest[count_new:]
    half_heads = k.shape[1] // DH // 2
    hbm = 3 if send else 0
    targets, staged, sems = rest[-4 - hbm : -4], rest[-4:-1], rest[-1]
    copies = []

    def place(other, first, count):
        half = 1 - core[0] if other else core[0]
        return pl.multiple_of((half * half_heads + first) * DH, DH)

    def write(other, first, count):
        c = pl.ds(place(other, first, count), count * DH)
        for m in range(3):
            copy = pltpu.make_async_copy(
                staged[m].at[:, c], targets[m].at[:, c], sems.at[len(copies)]
            )
            copy.start()
            copies.append(copy)

    for group in send:
        if group not in groups:
            write(*group)
    for group, both in zip(groups, states):
        start, count = place(*group), group[2]
        for i in range(count):
            c = pl.ds(pl.multiple_of(start + i * DH, DH), DH)
            before, behind = both[i].astype(BF16), both[count + i].astype(BF16)
            staged[0][:, c] = (dqi[:, c] + product(g[:, c], before, 1, 1)).astype(BF16)
            staged[1][:, c] = (dki[:, c] + product(v[:, c], behind, 1, 1)).astype(BF16)
            staged[2][:, c] = (dvi[:, c] + product(k[:, c], behind, 1, 0)).astype(BF16)
        if group in send:
            write(*group)
    for copy in copies:
        copy.wait()


def final(groups, send, core, args, local, states, outs, staged):
    _, k, v, g = args
    inputs = (core, k, v, g, *local, *states)
    filled = (*outs, *staged)
    shapes = [jax.ShapeDtypeStruct(k.shape, BF16)] * 3 if send else []
    shapes += [pltpu.VMEM(k.shape, BF16)] * 3
    behind = len(shapes) - len(filled)
    result = pl.pallas_call(
        functools.partial(final_kernel, groups, send),
        in_specs=[SMEM]
        + [VMEM] * (len(inputs) - 1)
        + [HBM] * len(outs)
        + [VMEM] * len(staged),
        out_specs=([HBM] * 3 if send else []) + [VMEM] * 3,
        out_shape=shapes,
        scratch_shapes=[pltpu.SemaphoreType.DMA((3 * max(len(send), 1),))],
        input_output_aliases={len(inputs) + i: behind + i for i in range(len(filled))},
        compiler_params=pltpu.CompilerParams(vmem_limit_bytes=8 << 20),
        name="final",
    )(*inputs, *filled)
    return result[:-3], result[-3:]


def after(values, *events):
    values = tuple(values)
    return lax.optimization_barrier(values + tuple(events))[: len(values)]


def swap(value):
    return lax.ppermute(value, "sub", [(0, 1), (1, 0)])


def exchange(value, chips, step):
    partner = {}
    for low in (step, chips - 2 - step):
        for core in (0, 1):
            a, b = 2 * low + core, 2 * low + 2 + core
            partner[a], partner[b] = b, a
    pairs = [(d, partner.get(d, d ^ 1)) for d in range(2 * chips)]
    return lax.ppermute(value, ("seq", "sub"), pairs)


def body(*args):
    chips = lax.axis_size("seq")
    core, chip = lax.axis_index("sub").astype(jnp.int32), lax.axis_index("seq")
    heads = args[0].shape[1] // DH
    chunks = min(CHUNKS, heads // 2)
    parts = tuple(
        heads // 2 * (c + 1) // chunks - heads // 2 * c // chunks for c in range(chunks)
    )
    slots = 1 + (chips - 2) * chunks
    plan = PLAN if (heads, slots) == (sum(PLAN), len(PLAN)) else (0,) * (slots - 1) + (heads,)
    at = [chip == c for c in range(chips)]
    core, first_core, *rest = lax.optimization_barrier((core.reshape(1), core == 0, *at, *args))
    at, args = rest[:chips], rest[chips:]
    given, args, keep, give = args, (), [], []
    for c, n in enumerate(parts):
        args, kept, gave = states(core, sum(parts[:c]), n, given, args)
        keep.append(kept)
        give.append(gave)
    got = [swap(x) for x in give]
    total = [None] * chunks
    local, done = (), 0

    def local_piece(count, event):
        nonlocal local, done
        if count:
            local = intra(done, count, *after(args, event), local)
            done += count
            event = local[0]
        return event

    prefix = [jnp.zeros_like(x[:n]) for x, n in zip(keep, parts)]
    suffix = list(prefix)
    arrived = [None] * chunks
    event, outs, staged, waiting, own, other = None, (), (), [], [], []
    for step in range(chips):
        if step == 1:
            event = local_piece(plan[0], event)
        for c, n in enumerate(parts):
            if step == 0:
                if c:
                    (got[c],) = after(got[c : c + 1], event)
                total[c] = keep[c] + got[c]
            else:
                (arrived[c],) = after(arrived[c : c + 1], event)
                prefix[c] = jnp.where(at[step], arrived[c], prefix[c])
                suffix[c] = jnp.where(at[chips - 1 - step], arrived[c], suffix[c])
            if step == chips - 1:
                zero = jnp.zeros_like(prefix[c])
                own.append(
                    jnp.concatenate(
                        [
                            prefix[c] + jnp.where(first_core, zero, got[c][:n]),
                            suffix[c] + jnp.where(first_core, got[c][n:], zero),
                        ]
                    )
                )
                lend = jnp.concatenate(
                    [
                        prefix[c] + jnp.where(first_core, keep[c][:n], zero),
                        suffix[c] + jnp.where(first_core, zero, keep[c][n:]),
                    ]
                )
                other.append(swap(lend))
                groups, use = [(False, sum(parts[:c]), n)], [own[c]]
                if c:
                    groups.append((True, sum(parts[: c - 1]), parts[c - 1]))
                    use.append(other[c - 1])
                send, waiting = (waiting, groups) if c else ([], groups)
                outs, staged = final(
                    tuple(groups), tuple(send), core, args, local, use, outs, staged
                )
                event = staged[0]
                continue
            sent = jnp.where(at[step], total[c][:n], total[c][n:])
            if step:
                sent = sent + arrived[c]
            arrived[c] = exchange(sent, chips, step)
            event = sent
            if step:
                event = local_piece(plan[1 + (step - 1) * chunks + c], sent)
    last_group = (True, sum(parts[:-1]), parts[-1])
    send = (*waiting, last_group)
    outs, _ = final((last_group,), send, core, args, local, other[-1:], outs, staged)
    return tuple(outs)


def solution(mesh):
    placed = P(("rep", "seq", "sub"), "head")
    return jax.shard_map(
        body, mesh=mesh, in_specs=(placed,) * 4, out_specs=(placed,) * 3, check_vma=False
    )
```

```python
import functools

import jax
import jax.numpy as jnp
from jax import lax
from jax.experimental import pallas as pl
from jax.experimental.pallas import tpu as pltpu
from jax.sharding import PartitionSpec as P

DH = 128
CHUNKS = 2
PLAN = (4, 1, 3, 0, 0)
F32 = jnp.float32
BF16 = jnp.bfloat16
VMEM = pl.BlockSpec(memory_space=pltpu.VMEM)
HBM = pl.BlockSpec(memory_space=pltpu.HBM)
SMEM = pl.BlockSpec(memory_space=pltpu.SMEM)


def product(left, right, left_axis, right_axis):
    return lax.dot_general(
        left, right, (((left_axis,), (right_axis,)), ((), ())), preferred_element_type=F32
    )


def head_columns(head):
    return slice(head * DH, (head + 1) * DH)


def states_kernel(parts, core, q_hbm, k_hbm, v_hbm, g_hbm, q, k, v, g, *rest):
    keep, give, sems = rest[: len(parts)], rest[len(parts) : 2 * len(parts)], rest[-1]
    width = q.shape[1] // 2
    loads = []
    for pair in (((k_hbm, k), (v_hbm, v)), ((q_hbm, q), (g_hbm, g))):
        for half in (0, 1):
            c = slice(half * width, (half + 1) * width)
            copies = [
                pltpu.make_async_copy(
                    source.at[:, c], target.at[:, c], sems.at[2 * len(loads) + i]
                )
                for i, (source, target) in enumerate(pair)
            ]
            loads.append(copies)
            for copy in copies:
                copy.start()

    def fill(outs, x, y, place, half):
        h = 0
        for out, count in zip(outs, parts):
            for i in range(count):
                c = slice(half * width + h * DH, half * width + (h + 1) * DH)
                out[place * count + i] = product(x[:, c], y[:, c], 0, 0)
                h += 1

    for n, copies in enumerate(loads):
        place, half = divmod(n, 2)
        x, y = ((k, v), (q, g))[place]
        for copy in copies:
            copy.wait()

        @pl.when(core[0] == half)
        def _():
            fill(keep, x, y, place, half)

        @pl.when(core[0] != half)
        def _():
            fill(give, x, y, place, half)


def states(core, parts, args):
    outs = [pltpu.VMEM((2 * n, DH, DH), F32) for n in parts] * 2
    result = pl.pallas_call(
        functools.partial(states_kernel, parts),
        in_specs=[SMEM] + [HBM] * 4,
        out_specs=[VMEM] * (4 + len(outs)),
        out_shape=[pltpu.VMEM(args[0].shape, BF16)] * 4 + outs,
        scratch_shapes=[pltpu.SemaphoreType.DMA((8,))],
        compiler_params=pltpu.CompilerParams(vmem_limit_bytes=8 << 20),
        name="states",
    )(core, *[pltpu.with_memory_space_constraint(x, pltpu.HBM) for x in args])
    return result[:4], list(result[4 : 4 + len(parts)]), list(result[4 + len(parts) :])


def intra_kernel(first, heads, q, k, v, g, *rest):
    dq, dk, dv = rest[-3:]
    rows = q.shape[0]
    row = lax.broadcasted_iota(jnp.int32, (rows, rows), 0)
    col = lax.broadcasted_iota(jnp.int32, (rows, rows), 1)
    for h in range(first, first + heads):
        c = head_columns(h)
        qh, kh, vh, gh = q[:, c], k[:, c], v[:, c], g[:, c]
        grad_scores = jnp.where(row >= col, product(gh, vh, 1, 1), 0.0).astype(BF16)
        dq[:, c] = product(grad_scores, kh, 1, 0)
        dk[:, c] = product(grad_scores, qh, 0, 0)
        attn_scores = jnp.where(row <= col, product(kh, qh, 1, 1), 0.0).astype(BF16)
        dv[:, c] = product(attn_scores, gh, 1, 0)


def intra(first, heads, q, k, v, g, filled):
    return pl.pallas_call(
        functools.partial(intra_kernel, first, heads),
        in_specs=[VMEM] * (4 + len(filled)),
        out_specs=[VMEM] * 3,
        out_shape=[pltpu.VMEM(q.shape, F32)] * 3,
        input_output_aliases={4 + i: i for i in range(len(filled))},
        compiler_params=pltpu.CompilerParams(vmem_limit_bytes=16 << 20),
        name="intra",
    )(q, k, v, g, *filled)


def final_kernel(groups, send, core, k, v, g, dqi, dki, dvi, *rest):
    count_new = len(groups)
    states, rest = rest[:count_new], rest[count_new:]
    half_heads = k.shape[1] // DH // 2
    hbm = 3 if send else 0
    targets, staged, sems = rest[-4 - hbm : -4], rest[-4:-1], rest[-1]
    copies = []

    def place(other, first, count):
        half = 1 - core[0] if other else core[0]
        return pl.multiple_of((half * half_heads + first) * DH, DH)

    def write(other, first, count):
        c = pl.ds(place(other, first, count), count * DH)
        for m in range(3):
            copy = pltpu.make_async_copy(
                staged[m].at[:, c], targets[m].at[:, c], sems.at[len(copies)]
            )
            copy.start()
            copies.append(copy)

    for group in send:
        if group not in groups:
            write(*group)
    for group, both in zip(groups, states):
        start, count = place(*group), group[2]
        for i in range(count):
            c = pl.ds(pl.multiple_of(start + i * DH, DH), DH)
            before, behind = both[i].astype(BF16), both[count + i].astype(BF16)
            staged[0][:, c] = (dqi[:, c] + product(g[:, c], before, 1, 1)).astype(BF16)
            staged[1][:, c] = (dki[:, c] + product(v[:, c], behind, 1, 1)).astype(BF16)
            staged[2][:, c] = (dvi[:, c] + product(k[:, c], behind, 1, 0)).astype(BF16)
        if group in send:
            write(*group)
    for copy in copies:
        copy.wait()


def final(groups, send, core, args, local, states, outs, staged):
    _, k, v, g = args
    inputs = (core, k, v, g, *local, *states)
    filled = (*outs, *staged)
    shapes = [jax.ShapeDtypeStruct(k.shape, BF16)] * 3 if send else []
    shapes += [pltpu.VMEM(k.shape, BF16)] * 3
    behind = len(shapes) - len(filled)
    result = pl.pallas_call(
        functools.partial(final_kernel, groups, send),
        in_specs=[SMEM]
        + [VMEM] * (len(inputs) - 1)
        + [HBM] * len(outs)
        + [VMEM] * len(staged),
        out_specs=([HBM] * 3 if send else []) + [VMEM] * 3,
        out_shape=shapes,
        scratch_shapes=[pltpu.SemaphoreType.DMA((3 * max(len(send), 1),))],
        input_output_aliases={len(inputs) + i: behind + i for i in range(len(filled))},
        compiler_params=pltpu.CompilerParams(vmem_limit_bytes=8 << 20),
        name="final",
    )(*inputs, *filled)
    return result[:-3], result[-3:]


def after(values, *events):
    values = tuple(values)
    return lax.optimization_barrier(values + tuple(events))[: len(values)]


def swap(value):
    return lax.ppermute(value, "sub", [(0, 1), (1, 0)])


def exchange(value, chips, step):
    partner = {}
    for low in (step, chips - 2 - step):
        for core in (0, 1):
            a, b = 2 * low + core, 2 * low + 2 + core
            partner[a], partner[b] = b, a
    pairs = [(d, partner.get(d, d ^ 1)) for d in range(2 * chips)]
    return lax.ppermute(value, ("seq", "sub"), pairs)


def body(*args):
    chips = lax.axis_size("seq")
    core, chip = lax.axis_index("sub").astype(jnp.int32), lax.axis_index("seq")
    heads = args[0].shape[1] // DH
    chunks = min(CHUNKS, heads // 2)
    parts = tuple(
        heads // 2 * (c + 1) // chunks - heads // 2 * c // chunks for c in range(chunks)
    )
    slots = 1 + (chips - 2) * chunks
    plan = PLAN if (heads, slots) == (sum(PLAN), len(PLAN)) else (0,) * (slots - 1) + (heads,)
    at = [chip == c for c in range(chips)]
    core, first_core, *rest = lax.optimization_barrier((core.reshape(1), core == 0, *at, *args))
    at, args = rest[:chips], rest[chips:]
    args, keep, give = states(core, parts, args)
    got = [swap(x) for x in give]
    total = [None] * chunks
    local, done = (), 0

    def local_piece(count, event):
        nonlocal local, done
        if count:
            local = intra(done, count, *after(args, event), local)
            done += count
            event = local[0]
        return event

    prefix = [jnp.zeros_like(x[:n]) for x, n in zip(keep, parts)]
    suffix = list(prefix)
    arrived = [None] * chunks
    event, outs, staged, waiting, own, other = None, (), (), [], [], []
    for step in range(chips):
        if step == 1:
            event = local_piece(plan[0], event)
        for c, n in enumerate(parts):
            if step == 0:
                if c:
                    (got[c],) = after(got[c : c + 1], event)
                total[c] = keep[c] + got[c]
            else:
                (arrived[c],) = after(arrived[c : c + 1], event)
                prefix[c] = jnp.where(at[step], arrived[c], prefix[c])
                suffix[c] = jnp.where(at[chips - 1 - step], arrived[c], suffix[c])
            if step == chips - 1:
                zero = jnp.zeros_like(prefix[c])
                own.append(
                    jnp.concatenate(
                        [
                            prefix[c] + jnp.where(first_core, zero, got[c][:n]),
                            suffix[c] + jnp.where(first_core, got[c][n:], zero),
                        ]
                    )
                )
                lend = jnp.concatenate(
                    [
                        prefix[c] + jnp.where(first_core, keep[c][:n], zero),
                        suffix[c] + jnp.where(first_core, zero, keep[c][n:]),
                    ]
                )
                other.append(swap(lend))
                groups, use = [(False, sum(parts[:c]), n)], [own[c]]
                if c:
                    groups.insert(0, (True, sum(parts[: c - 1]), parts[c - 1]))
                    use.insert(0, other[c - 1])
                send, waiting = ([*waiting, *groups[:-1]], groups[-1:]) if c else ([], groups)
                outs, staged = final(
                    tuple(groups), tuple(send), core, args, local, use, outs, staged
                )
                event = staged[0]
                continue
            sent = jnp.where(at[step], total[c][:n], total[c][n:])
            if step:
                sent = sent + arrived[c]
            arrived[c] = exchange(sent, chips, step)
            event = sent
            if step:
                event = local_piece(plan[1 + (step - 1) * chunks + c], sent)
    last_group = (True, sum(parts[:-1]), parts[-1])
    send = (*waiting, last_group)
    outs, _ = final((last_group,), send, core, args, local, other[-1:], outs, staged)
    return tuple(outs)


def solution(mesh):
    placed = P(("rep", "seq", "sub"), "head")
    return jax.shard_map(
        body, mesh=mesh, in_specs=(placed,) * 4, out_specs=(placed,) * 3, check_vma=False
    )
```

```python
import functools

import jax
import jax.numpy as jnp
from jax import lax
from jax.experimental import pallas as pl
from jax.experimental.pallas import tpu as pltpu
from jax.sharding import PartitionSpec as P

DH = 128
CHUNKS = 2
PLAN = (0, 1, 1, 2, 2, 2)
F32 = jnp.float32
BF16 = jnp.bfloat16
VMEM = pl.BlockSpec(memory_space=pltpu.VMEM)
HBM = pl.BlockSpec(memory_space=pltpu.HBM)
SMEM = pl.BlockSpec(memory_space=pltpu.SMEM)


def product(left, right, left_axis, right_axis):
    return lax.dot_general(
        left, right, (((left_axis,), (right_axis,)), ((), ())), preferred_element_type=F32
    )


def head_columns(head):
    return slice(head * DH, (head + 1) * DH)


def states_kernel(parts, later, place, q_hbm, k_hbm, v_hbm, g_hbm, *rest):
    q, k, v, g = rest[4 * later : 4 * later + 4]
    rest = rest[4 * later + 4 :]
    keep, give, sems = rest[: len(parts)], rest[len(parts) : 2 * len(parts)], rest[-1]
    width = q.shape[1] // 2

    def fill(outs, x, y, half):
        h = 0
        for out in outs:
            for i in range(out.shape[0]):
                c = slice(half * width + h * DH, half * width + (h + 1) * DH)
                out[i] = product(x[:, c], y[:, c], 0, 0)
                h += 1

    def run(x_hbm, y_hbm, x, y):
        loads = []
        for half in (0, 1):
            c = slice(half * width, (half + 1) * width)
            for i, (source, target) in enumerate(((x_hbm, x), (y_hbm, y))):
                loads.append(
                    pltpu.make_async_copy(
                        source.at[:, c], target.at[:, c], sems.at[2 * half + i]
                    )
                )
                loads[-1].start()
        for half in (0, 1):
            for copy in loads[2 * half : 2 * half + 2]:
                copy.wait()

            @pl.when(place[0] == half)
            def _():
                fill(keep, x, y, half)

            @pl.when(place[0] != half)
            def _():
                fill(give, x, y, half)

    @pl.when(place[1] == later)
    def _():
        run(k_hbm, v_hbm, k, v)

    @pl.when(place[1] != later)
    def _():
        run(q_hbm, g_hbm, q, g)


def states(place, parts, args, filled):
    outs = [pltpu.VMEM((n, DH, DH), F32) for n in parts] * 2
    result = pl.pallas_call(
        functools.partial(states_kernel, parts, 1 if filled else 0),
        in_specs=[SMEM] + [HBM] * 4 + [VMEM] * len(filled),
        out_specs=[VMEM] * (4 + len(outs)),
        out_shape=[pltpu.VMEM(args[0].shape, BF16)] * 4 + outs,
        scratch_shapes=[pltpu.SemaphoreType.DMA((4,))],
        input_output_aliases={5 + i: i for i in range(len(filled))},
        compiler_params=pltpu.CompilerParams(vmem_limit_bytes=8 << 20),
        name="states",
    )(place, *[pltpu.with_memory_space_constraint(x, pltpu.HBM) for x in args], *filled)
    return result[:4], list(result[4 : 4 + len(parts)]), list(result[4 + len(parts) :])


def intra_kernel(first, heads, q, k, v, g, *rest):
    dq, dk, dv = rest[-3:]
    rows = q.shape[0]
    top = rows // 2
    row = lax.broadcasted_iota(jnp.int32, (rows, top), 0)
    col = lax.broadcasted_iota(jnp.int32, (rows, top), 1)
    below = row >= col
    row = lax.broadcasted_iota(jnp.int32, (top, rows), 0)
    col = lax.broadcasted_iota(jnp.int32, (top, rows), 1)
    above = row <= col
    for h in range(first, first + heads):
        c = head_columns(h)
        qh, kh, vh, gh = q[:, c], k[:, c], v[:, c], g[:, c]
        q1, k0, k1, v0, v1, g1 = qh[top:], kh[:top], kh[top:], vh[:top], vh[top:], gh[top:]
        left = jnp.where(below, product(gh, v0, 1, 1), 0.0).astype(BF16)
        right = jnp.where(below[:top], product(g1, v1, 1, 1), 0.0).astype(BF16)
        dq[:top, c] = product(left[:top], k0, 1, 0)
        dq[top:, c] = product(jnp.concatenate([left[top:], right], axis=1), kh, 1, 0)
        dk[:top, c] = product(left, qh, 0, 0)
        dk[top:, c] = product(right, q1, 0, 0)
        upper = jnp.where(above, product(k0, qh, 1, 1), 0.0).astype(BF16)
        lower = jnp.where(above[:, :top], product(k1, q1, 1, 1), 0.0).astype(BF16)
        dv[:top, c] = product(upper, gh, 1, 0)
        dv[top:, c] = product(lower, g1, 1, 0)


def intra(first, heads, q, k, v, g, filled):
    return pl.pallas_call(
        functools.partial(intra_kernel, first, heads),
        in_specs=[VMEM] * (4 + len(filled)),
        out_specs=[VMEM] * 3,
        out_shape=[pltpu.VMEM(q.shape, F32)] * 3,
        input_output_aliases={4 + i: i for i in range(len(filled))},
        compiler_params=pltpu.CompilerParams(vmem_limit_bytes=16 << 20),
        name="intra",
    )(q, k, v, g, *filled)


def final_kernel(groups, send, core, k, v, g, dqi, dki, dvi, *rest):
    count_new = len(groups)
    states, rest = rest[:count_new], rest[count_new:]
    half_heads = k.shape[1] // DH // 2
    hbm = 3 if send else 0
    targets, staged, sems = rest[-4 - hbm : -4], rest[-4:-1], rest[-1]
    copies = []

    def place(other, first, count):
        half = 1 - core[0] if other else core[0]
        return pl.multiple_of((half * half_heads + first) * DH, DH)

    def write(other, first, count):
        c = pl.ds(place(other, first, count), count * DH)
        for m in range(3):
            copy = pltpu.make_async_copy(
                staged[m].at[:, c], targets[m].at[:, c], sems.at[len(copies)]
            )
            copy.start()
            copies.append(copy)

    for group in send:
        if group not in groups:
            write(*group)
    for group, both in zip(groups, states):
        owner, first, count = group
        start = place(*group)
        for i in range(count):
            c = pl.ds(pl.multiple_of(start + i * DH, DH), DH)
            before, behind = both[i].astype(BF16), both[count + i].astype(BF16)
            staged[0][:, c] = (dqi[:, c] + product(g[:, c], before, 1, 1)).astype(BF16)
            staged[1][:, c] = (dki[:, c] + product(v[:, c], behind, 1, 1)).astype(BF16)
            staged[2][:, c] = (dvi[:, c] + product(k[:, c], behind, 1, 0)).astype(BF16)
            if group in send:
                write(owner, first + i, 1)
    for copy in copies:
        copy.wait()


def final(groups, send, core, args, local, states, outs, staged):
    _, k, v, g = args
    inputs = (core, k, v, g, *local, *states)
    filled = (*outs, *staged)
    shapes = [jax.ShapeDtypeStruct(k.shape, BF16)] * 3 if send else []
    shapes += [pltpu.VMEM(k.shape, BF16)] * 3
    behind = len(shapes) - len(filled)
    result = pl.pallas_call(
        functools.partial(final_kernel, groups, send),
        in_specs=[SMEM]
        + [VMEM] * (len(inputs) - 1)
        + [HBM] * len(outs)
        + [VMEM] * len(staged),
        out_specs=([HBM] * 3 if send else []) + [VMEM] * 3,
        out_shape=shapes,
        scratch_shapes=[pltpu.SemaphoreType.DMA((3 * max(sum(count for _, _, count in send), 1),))],
        input_output_aliases={len(inputs) + i: behind + i for i in range(len(filled))},
        compiler_params=pltpu.CompilerParams(vmem_limit_bytes=8 << 20),
        name="final",
    )(*inputs, *filled)
    return result[:-3], result[-3:]


def after(values, *events):
    values = tuple(values)
    return lax.optimization_barrier(values + tuple(events))[: len(values)]


def swap(value):
    return lax.ppermute(value, "sub", [(0, 1), (1, 0)])


def exchange(value, chips, step):
    partner = {}
    for low in (step, chips - 2 - step):
        for core in (0, 1):
            a, b = 2 * low + core, 2 * low + 2 + core
            partner[a], partner[b] = b, a
    pairs = [(d, partner.get(d, d ^ 1)) for d in range(2 * chips)]
    return lax.ppermute(value, ("seq", "sub"), pairs)


def body(*args):
    chips = lax.axis_size("seq")
    core, chip = lax.axis_index("sub").astype(jnp.int32), lax.axis_index("seq")
    heads = args[0].shape[1] // DH
    chunks = min(CHUNKS, heads // 2)
    parts = tuple(
        heads // 2 * (c + 1) // chunks - heads // 2 * c // chunks for c in range(chunks)
    )
    slots = (chips - 1) * chunks
    plan = PLAN if (heads, slots) == (sum(PLAN), len(PLAN)) else (0,) * (slots - 1) + (heads,)
    early = chip < chips // 2
    same = (core == 0) == early
    place = jnp.stack([core, 1 - early.astype(jnp.int32)])
    at = [chip == c for c in range(chips)]
    core, place, first_core, same, *rest = lax.optimization_barrier(
        (core.reshape(1), place, core == 0, same, *at, *args)
    )
    at, given = rest[:chips], rest[chips:]
    args, keep, give = states(place, parts, given, ())
    got = [swap(x) for x in give]
    total = [None] * chunks
    local, done = (), 0

    def local_piece(count, event):
        nonlocal local, done
        if count:
            local = intra(done, count, *after(args, event), local)
            done += count
            event = local[0]
        return event

    prefix = [jnp.zeros_like(x[:n]) for x, n in zip(keep, parts)]
    suffix = list(prefix)
    arrived = [None] * chunks
    event, outs, staged, waiting, own, other = None, (), (), [], [], []
    for step in range(chips):
        for c, n in enumerate(parts):
            if step == 0:
                if c:
                    (got[c],) = after(got[c : c + 1], event)
                total[c] = keep[c] + got[c]
            else:
                (arrived[c],) = after(arrived[c : c + 1], event)
                prefix[c] = jnp.where(at[step], arrived[c], prefix[c])
                suffix[c] = jnp.where(at[chips - 1 - step], arrived[c], suffix[c])
            if step == chips // 2:
                total[c] = keep_late[c] + got_late[c]
            if step == chips - 1:
                zero = jnp.zeros_like(prefix[c])
                kept = jnp.where(same, keep[c], keep_late[c])
                gotten = jnp.where(same, got_late[c], got[c])
                own.append(
                    jnp.concatenate(
                        [
                            prefix[c] + jnp.where(first_core, zero, gotten),
                            suffix[c] + jnp.where(first_core, gotten, zero),
                        ]
                    )
                )
                lend = jnp.concatenate(
                    [
                        prefix[c] + jnp.where(first_core, kept, zero),
                        suffix[c] + jnp.where(first_core, zero, kept),
                    ]
                )
                other.append(swap(lend))
                groups, use = [(False, sum(parts[:c]), n)], [own[c]]
                if c:
                    groups.insert(0, (True, sum(parts[: c - 1]), parts[c - 1]))
                    use.insert(0, other[c - 1])
                send, waiting = ([*waiting, *groups[:-1]], groups[-1:]) if c else ([], groups)
                outs, staged = final(
                    tuple(groups), tuple(send), core, args, local, use, outs, staged
                )
                event = staged[0]
                continue
            sent = total[c] + arrived[c] if step else total[c]
            arrived[c] = exchange(sent, chips, step)
            event = sent
            if step == 0 and c == chunks - 1:
                args, keep_late, give_late = states(place, parts, given, after(args, event))
                got_late = [swap(x) for x in give_late]
                event = keep_late[0]
            event = local_piece(plan[step * chunks + c], event)
    last_group = (True, sum(parts[:-1]), parts[-1])
    send = (*waiting, last_group)
    outs, _ = final((last_group,), send, core, args, local, other[-1:], outs, staged)
    return tuple(outs)


def solution(mesh):
    placed = P(("rep", "seq", "sub"), "head")
    return jax.shard_map(
        body, mesh=mesh, in_specs=(placed,) * 4, out_specs=(placed,) * 3, check_vma=False
    )
```

```python
import functools

import jax
import jax.numpy as jnp
from jax import lax
from jax.experimental import pallas as pl
from jax.experimental.pallas import tpu as pltpu
from jax.sharding import PartitionSpec as P

DH = 128
CHUNKS = 2
PLAN = (0, 1, 1, 2, 2, 2)
F32 = jnp.float32
BF16 = jnp.bfloat16
VMEM = pl.BlockSpec(memory_space=pltpu.VMEM)
HBM = pl.BlockSpec(memory_space=pltpu.HBM)
SMEM = pl.BlockSpec(memory_space=pltpu.SMEM)


def product(left, right, left_axis, right_axis):
    return lax.dot_general(
        left, right, (((left_axis,), (right_axis,)), ((), ())), preferred_element_type=F32
    )


def head_columns(head):
    return slice(head * DH, (head + 1) * DH)


def states_kernel(parts, later, place, q_hbm, k_hbm, v_hbm, g_hbm, *rest):
    q, k, v, g = rest[4 * later : 4 * later + 4]
    rest = rest[4 * later + 4 :]
    keep, give, sems = rest[: len(parts)], rest[len(parts) : 2 * len(parts)], rest[-1]
    width = q.shape[1] // 2

    def fill(outs, x, y, half):
        h = 0
        for out in outs:
            for i in range(out.shape[0]):
                c = slice(half * width + h * DH, half * width + (h + 1) * DH)
                out[i] = product(x[:, c], y[:, c], 0, 0)
                h += 1

    def run(x_hbm, y_hbm, x, y):
        loads = [
            pltpu.make_async_copy(source, target, sems.at[i])
            for i, (source, target) in enumerate(((x_hbm, x), (y_hbm, y)))
        ]
        for copy in loads:
            copy.start()
        for copy in loads:
            copy.wait()

        @pl.when(place[0] == 0)
        def _():
            fill(give, x, y, 1)
            fill(keep, x, y, 0)

        @pl.when(place[0] != 0)
        def _():
            fill(give, x, y, 0)
            fill(keep, x, y, 1)

    @pl.when(place[1] == later)
    def _():
        run(k_hbm, v_hbm, k, v)

    @pl.when(place[1] != later)
    def _():
        run(q_hbm, g_hbm, q, g)


def states(place, parts, args, filled):
    outs = [pltpu.VMEM((n, DH, DH), F32) for n in parts] * 2
    result = pl.pallas_call(
        functools.partial(states_kernel, parts, 1 if filled else 0),
        in_specs=[SMEM] + [HBM] * 4 + [VMEM] * len(filled),
        out_specs=[VMEM] * (4 + len(outs)),
        out_shape=[pltpu.VMEM(args[0].shape, BF16)] * 4 + outs,
        scratch_shapes=[pltpu.SemaphoreType.DMA((2,))],
        input_output_aliases={5 + i: i for i in range(len(filled))},
        compiler_params=pltpu.CompilerParams(vmem_limit_bytes=8 << 20),
        name="states",
    )(place, *[pltpu.with_memory_space_constraint(x, pltpu.HBM) for x in args], *filled)
    return result[:4], list(result[4 : 4 + len(parts)]), list(result[4 + len(parts) :])


def intra_kernel(first, heads, q, k, v, g, *rest):
    dq, dk, dv = rest[-3:]
    rows = q.shape[0]
    top = rows // 2
    row = lax.broadcasted_iota(jnp.int32, (rows, top), 0)
    col = lax.broadcasted_iota(jnp.int32, (rows, top), 1)
    below = row >= col
    row = lax.broadcasted_iota(jnp.int32, (top, rows), 0)
    col = lax.broadcasted_iota(jnp.int32, (top, rows), 1)
    above = row <= col
    for h in range(first, first + heads):
        c = head_columns(h)
        qh, kh, vh, gh = q[:, c], k[:, c], v[:, c], g[:, c]
        q1, k0, k1, v0, v1, g1 = qh[top:], kh[:top], kh[top:], vh[:top], vh[top:], gh[top:]
        left = jnp.where(below, product(gh, v0, 1, 1), 0.0).astype(BF16)
        right = jnp.where(below[:top], product(g1, v1, 1, 1), 0.0).astype(BF16)
        dq[:top, c] = product(left[:top], k0, 1, 0)
        dq[top:, c] = product(jnp.concatenate([left[top:], right], axis=1), kh, 1, 0)
        dk[:top, c] = product(left, qh, 0, 0)
        dk[top:, c] = product(right, q1, 0, 0)
        upper = jnp.where(above, product(k0, qh, 1, 1), 0.0).astype(BF16)
        lower = jnp.where(above[:, :top], product(k1, q1, 1, 1), 0.0).astype(BF16)
        dv[:top, c] = product(upper, gh, 1, 0)
        dv[top:, c] = product(lower, g1, 1, 0)


def intra(first, heads, q, k, v, g, filled):
    return pl.pallas_call(
        functools.partial(intra_kernel, first, heads),
        in_specs=[VMEM] * (4 + len(filled)),
        out_specs=[VMEM] * 3,
        out_shape=[pltpu.VMEM(q.shape, F32)] * 3,
        input_output_aliases={4 + i: i for i in range(len(filled))},
        compiler_params=pltpu.CompilerParams(vmem_limit_bytes=16 << 20),
        name="intra",
    )(q, k, v, g, *filled)


def final_kernel(groups, send, core, k, v, g, dqi, dki, dvi, *rest):
    count_new = len(groups)
    states, rest = rest[:count_new], rest[count_new:]
    half_heads = k.shape[1] // DH // 2
    hbm = 3 if send else 0
    targets, staged, sems = rest[-4 - hbm : -4], rest[-4:-1], rest[-1]
    copies = []

    def place(other, first, count):
        half = 1 - core[0] if other else core[0]
        return pl.multiple_of((half * half_heads + first) * DH, DH)

    def write(other, first, count):
        c = pl.ds(place(other, first, count), count * DH)
        for m in range(3):
            copy = pltpu.make_async_copy(
                staged[m].at[:, c], targets[m].at[:, c], sems.at[len(copies)]
            )
            copy.start()
            copies.append(copy)

    for group in send:
        if group not in groups:
            write(*group)
    for group, both in zip(groups, states):
        owner, first, count = group
        start = place(*group)
        for i in range(count):
            c = pl.ds(pl.multiple_of(start + i * DH, DH), DH)
            before, behind = both[i].astype(BF16), both[count + i].astype(BF16)
            staged[0][:, c] = (dqi[:, c] + product(g[:, c], before, 1, 1)).astype(BF16)
            staged[1][:, c] = (dki[:, c] + product(v[:, c], behind, 1, 1)).astype(BF16)
            staged[2][:, c] = (dvi[:, c] + product(k[:, c], behind, 1, 0)).astype(BF16)
            if group in send:
                write(owner, first + i, 1)
    for copy in copies:
        copy.wait()


def final(groups, send, core, args, local, states, outs, staged):
    _, k, v, g = args
    inputs = (core, k, v, g, *local, *states)
    filled = (*outs, *staged)
    shapes = [jax.ShapeDtypeStruct(k.shape, BF16)] * 3 if send else []
    shapes += [pltpu.VMEM(k.shape, BF16)] * 3
    behind = len(shapes) - len(filled)
    result = pl.pallas_call(
        functools.partial(final_kernel, groups, send),
        in_specs=[SMEM]
        + [VMEM] * (len(inputs) - 1)
        + [HBM] * len(outs)
        + [VMEM] * len(staged),
        out_specs=([HBM] * 3 if send else []) + [VMEM] * 3,
        out_shape=shapes,
        scratch_shapes=[pltpu.SemaphoreType.DMA((3 * max(sum(count for _, _, count in send), 1),))],
        input_output_aliases={len(inputs) + i: behind + i for i in range(len(filled))},
        compiler_params=pltpu.CompilerParams(vmem_limit_bytes=8 << 20),
        name="final",
    )(*inputs, *filled)
    return result[:-3], result[-3:]


def after(values, *events):
    values = tuple(values)
    return lax.optimization_barrier(values + tuple(events))[: len(values)]


def swap(value):
    return lax.ppermute(value, "sub", [(0, 1), (1, 0)])


def exchange(value, chips, step):
    partner = {}
    for low in (step, chips - 2 - step):
        for core in (0, 1):
            a, b = 2 * low + core, 2 * low + 2 + core
            partner[a], partner[b] = b, a
    pairs = [(d, partner.get(d, d ^ 1)) for d in range(2 * chips)]
    return lax.ppermute(value, ("seq", "sub"), pairs)


def body(*args):
    chips = lax.axis_size("seq")
    core, chip = lax.axis_index("sub").astype(jnp.int32), lax.axis_index("seq")
    heads = args[0].shape[1] // DH
    chunks = min(CHUNKS, heads // 2)
    parts = tuple(
        heads // 2 * (c + 1) // chunks - heads // 2 * c // chunks for c in range(chunks)
    )
    slots = (chips - 1) * chunks
    plan = PLAN if (heads, slots) == (sum(PLAN), len(PLAN)) else (0,) * (slots - 1) + (heads,)
    early = chip < chips // 2
    same = (core == 0) == early
    place = jnp.stack([core, 1 - early.astype(jnp.int32)])
    at = [chip == c for c in range(chips)]
    core, place, first_core, same, *rest = lax.optimization_barrier(
        (core.reshape(1), place, core == 0, same, *at, *args)
    )
    at, given = rest[:chips], rest[chips:]
    args, keep, give = states(place, parts, given, ())
    got = [swap(x) for x in give]
    total = [None] * chunks
    local, done = (), 0

    def local_piece(count, event):
        nonlocal local, done
        if count:
            local = intra(done, count, *after(args, event), local)
            done += count
            event = local[0]
        return event

    prefix = [jnp.zeros_like(x[:n]) for x, n in zip(keep, parts)]
    suffix = list(prefix)
    arrived = [None] * chunks
    event, outs, staged, waiting, own, other = None, (), (), [], [], []
    for step in range(chips):
        for c, n in enumerate(parts):
            if step == 0:
                if c:
                    (got[c],) = after(got[c : c + 1], event)
                total[c] = keep[c] + got[c]
            else:
                (arrived[c],) = after(arrived[c : c + 1], event)
                prefix[c] = jnp.where(at[step], arrived[c], prefix[c])
                suffix[c] = jnp.where(at[chips - 1 - step], arrived[c], suffix[c])
            if step == chips // 2:
                total[c] = keep_late[c] + got_late[c]
            if step == chips - 1:
                zero = jnp.zeros_like(prefix[c])
                kept = jnp.where(same, keep[c], keep_late[c])
                gotten = jnp.where(same, got_late[c], got[c])
                own.append(
                    jnp.concatenate(
                        [
                            prefix[c] + jnp.where(first_core, zero, gotten),
                            suffix[c] + jnp.where(first_core, gotten, zero),
                        ]
                    )
                )
                lend = jnp.concatenate(
                    [
                        prefix[c] + jnp.where(first_core, kept, zero),
                        suffix[c] + jnp.where(first_core, zero, kept),
                    ]
                )
                other.append(swap(lend))
                groups, use = [(False, sum(parts[:c]), n)], [own[c]]
                if c:
                    groups.insert(0, (True, sum(parts[: c - 1]), parts[c - 1]))
                    use.insert(0, other[c - 1])
                send, waiting = ([*waiting, *groups[:-1]], groups[-1:]) if c else ([], groups)
                outs, staged = final(
                    tuple(groups), tuple(send), core, args, local, use, outs, staged
                )
                event = staged[0]
                continue
            sent = total[c] + arrived[c] if step else total[c]
            arrived[c] = exchange(sent, chips, step)
            event = sent
            if step == 0 and c == chunks - 1:
                args, keep_late, give_late = states(place, parts, given, after(args, event))
                got_late = [swap(x) for x in give_late]
                event = keep_late[0]
            event = local_piece(plan[step * chunks + c], event)
    last_group = (True, sum(parts[:-1]), parts[-1])
    send = (*waiting, last_group)
    outs, _ = final((last_group,), send, core, args, local, other[-1:], outs, staged)
    return tuple(outs)


def solution(mesh):
    placed = P(("rep", "seq", "sub"), "head")
    return jax.shard_map(
        body, mesh=mesh, in_specs=(placed,) * 4, out_specs=(placed,) * 3, check_vma=False
    )
```
